32 devices in a mesh: group: 4 (over x, core), member: 8 (over z, y).
Axes of the slice: x: 2, y: 2, z: 4, core: 2. Of those that a mesh axis runs over, the one named last changes fastest.
Arguments:
- activations: bfloat16 [8192, 1152], P(('group', 'member')), may hold values from -6 to 6
- routes: int32 [8192, 1], P(('group', 'member')), may hold values from 0 to 31; in each aligned block of 256 rows (0 to 255, 256 to 511, ...) at most 16 rows name the same one
- centre_bias: float32 [1152], replicated, may hold values from -2 to 2
- centre_first: float32 [1152], replicated, may hold values from -600 to 600
- centre_second: float32 [1152], replicated, may hold values from 1000 to 1000000
- router: bfloat16 [32, 1152], P(('group', 'member')), may hold values from -0.1875 to 0.1875
- router_first: float32 [32, 1152], P(('group', 'member')), may hold values from -180 to 180
- router_second: float32 [32, 1152], P(('group', 'member')), may hold values from 100 to 100000
- encoder: bfloat16 [32, 1152, 512], P(('group', 'member')), may hold values from -0.1875 to 0.1875
- enc_bias: float32 [32, 512], P(('group', 'member')), may hold values from -3 to 3
- decoder: bfloat16 [32, 512, 1152], P(('group', 'member')), may hold values from -0.25 to 0.25
- encoder_first: float32 [32, 1152, 512], P(('group', 'member')), may hold values from -30 to 30
- encoder_second: float32 [32, 1152, 512], P(('group', 'member')), may hold values from 1 to 1000
- enc_bias_first: float32 [32, 512], P(('group', 'member')), may hold values from -60 to 60
- enc_bias_second: float32 [32, 512], P(('group', 'member')), may hold values from 10 to 10000
- decoder_first: float32 [32, 512, 1152], P(('group', 'member')), may hold values from -30 to 30
- decoder_second: float32 [32, 512, 1152], P(('group', 'member')), may hold values from 1 to 1000
Outputs:
- recon: bfloat16 [8192, 1152], P(('group', 'member'))
- new_centre: float32 [1152], replicated
- new_centre_first: float32 [1152], replicated
- new_centre_second: float32 [1152], replicated
- new_router: bfloat16 [32, 1152], P(('group', 'member'))
- new_router_first: float32 [32, 1152], P(('group', 'member'))
- new_router_second: float32 [32, 1152], P(('group', 'member'))
- new_encoder: bfloat16 [32, 1152, 512], P(('group', 'member'))
- new_enc_bias: float32 [32, 512], P(('group', 'member'))
- new_decoder: bfloat16 [32, 512, 1152], P(('group', 'member'))
- new_encoder_first: float32 [32, 1152, 512], P(('group', 'member'))
- new_encoder_second: float32 [32, 1152, 512], P(('group', 'member'))
- new_enc_bias_first: float32 [32, 512], P(('group', 'member'))
- new_enc_bias_second: float32 [32, 512], P(('group', 'member'))
- new_decoder_first: float32 [32, 512, 1152], P(('group', 'member'))
- new_decoder_second: float32 [32, 512, 1152], P(('group', 'member'))
The draws below stay inside these ranges and needn't reach their ends.
Inputs may be any that keep to these rules, and one draw needn't show every extreme that they name: `routes`: each row names the one expert that serves it. At most 16 rows of one device name the same expert, and in every draw some device's rows name some expert exactly 16 times.
All inputs are finite; a program needn't handle non-finite values.
Results may differ from the reference program's by a relative error of at most 0.009.
Values may be sent and summed in bfloat16 or wider, within the bound.
A program may use at most 128 MiB of HBM per device.

```python
import math
import jax
import jax.numpy as jnp
import numpy as np
from jax import lax

D = 1152
LATENTS = 512
STEP = 10
TOK_DEV = 256
EXPERTS = 32
CAP = 16
TOKENS = 8192
N_GROUP = 4
N_MEMBER = 8


def block_scale(own_key, shape, cuts, least, high):
    level = 1.0
    for dim, parts in cuts:
        heights = jax.random.uniform(jax.random.fold_in(jax.random.fold_in(own_key, 6), dim), (parts,), jnp.float32, least / len(cuts), high / len(cuts))
        level = level * jnp.repeat(jnp.exp(heights), shape[dim] // parts).reshape((-1,) + (1,) * (len(shape) - 1 - dim))
    return level


def deal_out(own_key, own, number, rows, amount, top, limit, lean):
    sequence = jax.random.permutation(own_key, amount)
    packed, common = shares(amount, rows * top, limit, lean, True), shares(amount, rows * top, limit, lean, False)
    places = jnp.arange(amount)

    def named(lengths, rotation):
        used = int((lengths > 0).sum())
        fixed = max(1, used // 4)
        moved = fixed + (places - fixed + rotation * (used - fixed)) % max(1, amount - fixed)
        return jnp.zeros((amount,), jnp.int32).at[sequence[jnp.where(places < fixed, places, moved)]].set(jnp.asarray(lengths, jnp.int32))

    lengths = jnp.where(number % 4 == 0, named(packed, number // 4), named(common, number - number // 4 - 1))
    mixed = jax.random.permutation(jax.random.fold_in(own, 3), amount)
    source_of, receiver = mixed[0:amount // 2 * 2:2], mixed[1:amount // 2 * 2:2]
    margin = jnp.minimum(lengths[source_of] - 1, limit - lengths[receiver]) // 2
    margin = jnp.where((source_of == sequence[0]) | (receiver == sequence[0]) | (lengths[receiver] == 0), 0, jnp.maximum(margin, 0))
    moved = jax.random.randint(jax.random.fold_in(own, 4), (amount // 2,), 0, 1 << 20) % (margin + 1)
    lengths = lengths.at[source_of].add(-moved).at[receiver].add(moved)
    items = jnp.searchsorted(jnp.cumsum(lengths), jnp.arange(rows * top), side="right").astype(jnp.int32)
    grid = items.reshape(top, rows).T
    grid = grid[jax.random.permutation(jax.random.fold_in(own, 1), rows)]
    rotation = jax.random.randint(jax.random.fold_in(own, 2), (rows, 1), 0, top)
    return jnp.take_along_axis(grid, (jnp.arange(top)[None, :] + rotation) % top, axis=1)


def shares(number_of, total, bound, slope, full):
    weights = [(1 << 20) // math.isqrt(standing ** slope) + 1 for standing in range(1, number_of + 1)]
    largest = bound if full else min(bound, max(-(-total // number_of), total * weights[0] // sum(weights)))
    least = 1 if total - largest >= number_of - 1 else 0
    given, rest = [largest] + [least] * (number_of - 1), total - largest - least * (number_of - 1)
    while rest > 0:
        candidates = [i for i in range(1, number_of) if given[i] < largest] or [i for i in range(1, number_of) if given[i] < bound]
        whole, left = sum([weights[i] for i in candidates]), rest
        for i in candidates:
            more = min(bound - given[i], max(1, left * weights[i] // whole), rest)
            given[i] = given[i] + more
            rest = rest - more
    return np.array(given)


def scatter_about(key, extent, scale, limit, shards=(), held_as=jnp.bfloat16):
    factor_of = block_scale(key, extent, shards, -0.22, 0.18) if shards else 1.0
    array = jax.random.normal(key, extent, jnp.float32) * scale * factor_of
    return jnp.minimum(jnp.maximum(array, -limit), limit).astype(held_as)


def setup_inputs(seed: int = 0) -> dict:
    key_of = jax.random.split(jax.random.key(seed), 18)
    activations = scatter_about(key_of[0], (TOKENS, D), 1.0, 6.0, ((0, 32),))
    routes_keys = jax.random.split(jax.random.fold_in(key_of[1], 1), TOKENS // TOK_DEV)
    routes_turns = jax.random.permutation(jax.random.fold_in(key_of[1], 3), TOKENS // TOK_DEV)
    routes = jax.vmap(lambda own, number: deal_out(jax.random.fold_in(key_of[1], 2), own, number, TOK_DEV, EXPERTS, 1, CAP, 2))(routes_keys, routes_turns).reshape((TOKENS, 1))
    centre_bias = scatter_about(key_of[2], (D,), 0.3, 2.0, (), jnp.float32)
    centre_first = scatter_about(key_of[3], (D,), 100.0, 600.0, (), jnp.float32)
    centre_second = jnp.clip(jnp.exp(jax.random.uniform(key_of[4], (D,), jnp.float32, math.log(1000.0), math.log(1000000))), 1000.0, 1000000)
    router = scatter_about(key_of[5], (EXPERTS, D), D ** -0.5, 0.1875, ((0, 32),))
    router_first = scatter_about(key_of[6], (EXPERTS, D), 30.0, 180.0, ((0, 32),), jnp.float32)
    router_second = jnp.clip(jnp.exp(math.log(100000.0) - 6.9077553 * jax.random.uniform(key_of[7], (EXPERTS, D), jnp.float32) ** block_scale(key_of[7], (EXPERTS, D), ((0, 32),), -0.2, 0.2)), 100.0, 100000.0)
    encoder = scatter_about(key_of[8], (EXPERTS, D, LATENTS), D ** -0.5, 0.1875, ((0, 32),))
    enc_bias = scatter_about(key_of[9], (EXPERTS, LATENTS), 0.5, 3.0, ((0, 32),), jnp.float32)
    decoder = scatter_about(key_of[10], (EXPERTS, LATENTS, D), LATENTS ** -0.5, 0.25, ((0, 32),))
    encoder_first = scatter_about(key_of[11], (EXPERTS, D, LATENTS), 5.0, 30.0, ((0, 32),), jnp.float32)
    encoder_second = jnp.clip(jnp.exp(math.log(1000.0) - 6.9077553 * jax.random.uniform(key_of[12], (EXPERTS, D, LATENTS), jnp.float32) ** block_scale(key_of[12], (EXPERTS, D, LATENTS), ((0, 32),), -0.2, 0.2)), 1.0, 1000.0)
    enc_bias_first = scatter_about(key_of[13], (EXPERTS, LATENTS), 10.0, 60.0, ((0, 32),), jnp.float32)
    enc_bias_second = jnp.clip(jnp.exp(math.log(10000.0) - 6.9077553 * jax.random.uniform(key_of[14], (EXPERTS, LATENTS), jnp.float32) ** block_scale(key_of[14], (EXPERTS, LATENTS), ((0, 32),), -0.2, 0.2)), 10.0, 10000.0)
    decoder_first = scatter_about(key_of[15], (EXPERTS, LATENTS, D), 5.0, 30.0, ((0, 32),), jnp.float32)
    decoder_second = jnp.clip(jnp.exp(math.log(1000.0) - 6.9077553 * jax.random.uniform(key_of[16], (EXPERTS, LATENTS, D), jnp.float32) ** block_scale(key_of[16], (EXPERTS, LATENTS, D), ((0, 32),), -0.2, 0.2)), 1.0, 1000.0)
    return {"activations": activations, "routes": routes, "centre_bias": centre_bias, "centre_first": centre_first, "centre_second": centre_second, "router": router, "router_first": router_first, "router_second": router_second, "encoder": encoder, "enc_bias": enc_bias, "decoder": decoder, "encoder_first": encoder_first, "encoder_second": encoder_second, "enc_bias_first": enc_bias_first, "enc_bias_second": enc_bias_second, "decoder_first": decoder_first, "decoder_second": decoder_second}


learn_rate = 0.001
beta_one = 0.9
beta_two = 0.999
adam_eps = 1e-08
sparsity = 0.1

def adam_update(weights_in, gradient, moment_one, moment_two):
    first_new = beta_one * moment_one + (1.0 - beta_one) * gradient
    second_new = beta_two * moment_two + (1.0 - beta_two) * gradient * gradient
    first_hat = first_new / (1.0 - beta_one ** STEP)
    second_hat = second_new / (1.0 - beta_two ** STEP)
    stepped = weights_in.astype(jnp.float32) - learn_rate * first_hat / (jnp.sqrt(second_hat) + adam_eps)
    return (stepped.astype(weights_in.dtype), first_new, second_new)

def expert_pass(in_rows, live_mask, centre_bias, router_row, encoder, enc_bias, decoder):
    wide_rows = in_rows.astype(jnp.float32)
    centred = (wide_rows - centre_bias).astype(jnp.bfloat16)
    preact = jnp.dot(centred, encoder, preferred_element_type=jnp.float32) + enc_bias
    positive = jnp.maximum(preact, 0.0)
    latents = (positive * positive).astype(jnp.bfloat16)
    logits = jnp.dot(in_rows, router_row, preferred_element_type=jnp.float32)
    gating = jax.nn.sigmoid(logits)
    ungated = jnp.dot(latents, decoder, preferred_element_type=jnp.float32)
    rebuilt = centre_bias + gating[:, None] * ungated
    errors = (wide_rows - rebuilt) * live_mask[:, None]
    backward = (-gating[:, None] * errors).astype(jnp.bfloat16)
    decoder_grad = jnp.dot(latents.T, backward, preferred_element_type=jnp.float32)
    latent_grad = jnp.dot(backward, decoder.T, preferred_element_type=jnp.float32) + sparsity
    preact_grad = (latent_grad * 2.0 * positive * live_mask[:, None]).astype(jnp.bfloat16)
    encoder_grad = jnp.dot(centred.T, preact_grad, preferred_element_type=jnp.float32)
    bias_grad = lax.optimization_barrier(jnp.sum(preact_grad.astype(jnp.float32), axis=0))
    logit_grad = (-lax.optimization_barrier(jnp.sum(errors * ungated, axis=1)) * gating * (1.0 - gating)).astype(jnp.bfloat16)
    router_grad = jnp.dot(logit_grad, in_rows, preferred_element_type=jnp.float32)
    centre_part = -lax.optimization_barrier(jnp.sum(errors, axis=0)) - jnp.dot(encoder.astype(jnp.float32), bias_grad, precision=lax.Precision.HIGHEST)
    return (rebuilt.astype(jnp.bfloat16), (encoder_grad, bias_grad, decoder_grad, router_grad), centre_part)

def reference(activations, routes, centre_bias, centre_first, centre_second, router, router_first, router_second, encoder, enc_bias, decoder, encoder_first, encoder_second, enc_bias_first, enc_bias_second, decoder_first, decoder_second):
    experts = N_GROUP * N_MEMBER
    max_rows = experts * CAP
    tokens = activations.shape[0]
    route_ids = routes[:, 0]

    def per_expert(state_pair, expert_in):
        recon_all, centre_sum = state_pair
        expert_id, router_row, expert_encoder, expert_bias, expert_decoder, moments_in = expert_in
        is_mine = route_ids == expert_id
        row_index = jnp.nonzero(is_mine, size=max_rows, fill_value=0)[0].astype(jnp.int32)
        live_count = jnp.sum(is_mine.astype(jnp.int32))
        live_mask = (jnp.arange(max_rows).astype(jnp.int32) < live_count).astype(jnp.float32)
        in_rows = activations[row_index]
        rebuilt, grads, centre_part = expert_pass(in_rows, live_mask, centre_bias, router_row, expert_encoder, expert_bias, expert_decoder)
        target = jnp.where(live_mask > 0, row_index, tokens).astype(jnp.int32)
        recon_all = recon_all.at[target].set(rebuilt, mode='drop')
        router_new = adam_update(router_row, grads[3], moments_in[0], moments_in[1])
        encoder_new = adam_update(expert_encoder, grads[0], moments_in[2], moments_in[3])
        bias_new = adam_update(expert_bias, grads[1], moments_in[4], moments_in[5])
        decoder_new = adam_update(expert_decoder, grads[2], moments_in[6], moments_in[7])
        return ((recon_all, centre_sum + centre_part), (router_new, encoder_new, bias_new, decoder_new))
    zero_recon = jnp.zeros((tokens, activations.shape[1]), jnp.bfloat16)
    zero_centre = jnp.zeros((activations.shape[1],), jnp.float32)
    expert_ids = jnp.arange(experts).astype(jnp.int32)
    moments_all = (router_first, router_second, encoder_first, encoder_second, enc_bias_first, enc_bias_second, decoder_first, decoder_second)
    (recon_all, centre_grad), stacked = lax.scan(per_expert, (zero_recon, zero_centre), (expert_ids, router, encoder, enc_bias, decoder, moments_all))
    router_new, encoder_new, bias_new, decoder_new = stacked
    centre_new = adam_update(centre_bias, centre_grad, centre_first, centre_second)
    return (recon_all, centre_new[0], centre_new[1], centre_new[2], router_new[0], router_new[1], router_new[2], encoder_new[0], bias_new[0], decoder_new[0], encoder_new[1], encoder_new[2], bias_new[1], bias_new[2], decoder_new[1], decoder_new[2])
```

```python
import functools

import jax
import jax.numpy as jnp
from jax import lax
from jax.experimental import pallas as pl
from jax.experimental.pallas import tpu as pltpu
from jax.sharding import PartitionSpec as P

MESH = pl.DeviceIdType.MESH

STEP = 10


learn_rate = 0.001
beta_one = 0.9
beta_two = 0.999
adam_eps = 1e-08
sparsity = 0.1
EMPTY = 16.0
VMEM_LIMIT = 40 << 20
HELD_BLOCKS = 4


def adam_update(weights_in, gradient, moment_one, moment_two):
    first_new = beta_one * moment_one + (1.0 - beta_one) * gradient
    second_new = beta_two * moment_two + (1.0 - beta_two) * gradient * gradient
    first_hat = first_new / (1.0 - beta_one**STEP)
    second_hat = second_new / (1.0 - beta_two**STEP)
    stepped = weights_in.astype(jnp.float32) - learn_rate * first_hat / (
        jnp.sqrt(second_hat) + adam_eps
    )
    return (stepped.astype(weights_in.dtype), first_new, second_new)


def forward_pass(in_rows, centre_bias, router_row, encoder, enc_bias, decoder):
    centred = (in_rows.astype(jnp.float32) - centre_bias).astype(jnp.bfloat16)
    preact = jnp.dot(centred, encoder, preferred_element_type=jnp.float32) + enc_bias
    positive = jnp.maximum(preact, 0.0)
    latents = (positive * positive).astype(jnp.bfloat16)
    router_wide = jnp.broadcast_to(router_row[:, None], (router_row.shape[0], 128))
    logits = jnp.dot(in_rows, router_wide, preferred_element_type=jnp.float32)[:, 0]
    gating = jax.nn.sigmoid(logits)
    ungated = jnp.dot(latents, decoder, preferred_element_type=jnp.float32)
    rebuilt = centre_bias + gating[:, None] * ungated
    return (centred, positive, latents, gating, ungated, rebuilt)


def backward_pass(
    in_rows, live_mask, centred, positive, latents, gating, ungated, rebuilt, encoder, decoder
):
    errors = (in_rows.astype(jnp.float32) - rebuilt) * live_mask[:, None]
    backward = (-gating[:, None] * errors).astype(jnp.bfloat16)
    decoder_grad = jnp.dot(latents.T, backward, preferred_element_type=jnp.float32)
    latent_grad = jnp.dot(backward, decoder.T, preferred_element_type=jnp.float32) + sparsity
    preact_grad = (latent_grad * 2.0 * positive * live_mask[:, None]).astype(jnp.bfloat16)
    encoder_grad = jnp.dot(centred.T, preact_grad, preferred_element_type=jnp.float32)
    bias_grad = jnp.sum(preact_grad.astype(jnp.float32), axis=0)
    logit_grad = (-jnp.sum(errors * ungated, axis=1) * gating * (1.0 - gating)).astype(jnp.bfloat16)
    router_grad = jnp.dot(logit_grad, in_rows, preferred_element_type=jnp.float32)
    centre_part = -jnp.sum(errors, axis=0) - jnp.dot(
        encoder.astype(jnp.float32), bias_grad, precision=lax.Precision.HIGHEST
    )
    return (encoder_grad, bias_grad, decoder_grad, router_grad, centre_part)


def flipped(index, bits):
    result, place = index, 1
    while place <= bits:
        if bits & place:
            result = result + (1 - 2 * lax.rem(lax.div(index, place), 2)) * place
        place *= 2
    return result


def partner_of(offset, members):
    return (
        flipped(lax.axis_index("group"), offset // members),
        flipped(lax.axis_index("member"), offset % members),
    )


def greet(devices, members):
    barrier = pltpu.get_barrier_semaphore()
    for offset in range(1, devices):
        pl.semaphore_signal(
            barrier, inc=1, device_id=partner_of(offset, members), device_id_type=MESH
        )
    pl.semaphore_wait(barrier, devices - 1)


def dispatch_order(devices, members):
    half = members // 2
    near = [offset for offset in range(devices) if not offset & half]
    return near + [offset + half for offset in near]


IN_NAMES = (
    "x",
    "routes",
    "centre",
    "centre_m",
    "centre_v",
    "router",
    "router_m",
    "router_v",
    "encoder",
    "bias",
    "decoder",
    "em",
    "ev",
    "bias_m",
    "bias_v",
    "dm",
    "dv",
)
OUT_NAMES = (
    "o_recon",
    "o_centre",
    "o_centre_m",
    "o_centre_v",
    "o_router",
    "o_router_m",
    "o_router_v",
    "o_encoder",
    "o_bias",
    "o_decoder",
    "o_encoder_m",
    "o_encoder_v",
    "o_bias_m",
    "o_bias_v",
    "o_decoder_m",
    "o_decoder_v",
)
SCRATCH_NAMES = (
    "select",
    "packed",
    "arrived",
    "outgoing",
    "returned",
    "centred_buf",
    "latents_buf",
    "backward_buf",
    "preact_buf",
    "recon_acc",
    "part_buf",
    "part_in",
    "local_sem",
    "send_sem",
    "recv_sem",
    "back_send",
    "back_recv",
    "part_send",
    "part_recv",
)
REF_NAMES = (
    tuple(name + "_in" for name in IN_NAMES)
    + OUT_NAMES
    + IN_NAMES
    + SCRATCH_NAMES
)
LOAD_ORDER = (
    "routes",
    "x",
    "encoder",
    "decoder",
    "centre",
    "router",
    "bias",
    "dm",
    "dv",
    "em",
    "ev",
    "router_m",
    "router_v",
    "bias_m",
    "bias_v",
    "centre_m",
    "centre_v",
)


def adam_step(weights, gradient, moment_one, moment_two):
    first_new = beta_one * moment_one + (1.0 - beta_one) * gradient
    second_new = beta_two * moment_two + (1.0 - beta_two) * (gradient * gradient)
    scaled = first_new * (learn_rate / (1.0 - beta_one**STEP))
    root = jnp.sqrt(second_new * (1.0 / (1.0 - beta_two**STEP))) + adam_eps
    return (weights.astype(jnp.float32) - scaled / root, first_new, second_new)


def whole_kernel(devices, members, slot_cap, *refs):
    r = dict(zip(REF_NAMES, refs, strict=True))
    order = dispatch_order(devices, members)
    per_chunk = max(1, 128 // slot_cap)
    chunk_starts = list(range(0, devices, per_chunk))
    features = r["x"].shape[1]
    latent_count = r["latents_buf"].shape[1]
    row_count = r["x"].shape[0]

    def index_of(offset):
        group, member = partner_of(offset, members)
        return group * members + member

    barrier = pltpu.get_barrier_semaphore()
    for offset in range(1, devices):
        pl.semaphore_signal(
            barrier, inc=1, device_id=partner_of(offset, members), device_id_type=MESH
        )
    loads = {}
    for number, name in enumerate(LOAD_ORDER):
        loads[name] = pltpu.make_async_copy(r[name + "_in"], r[name], r["local_sem"].at[number])
        loads[name].start()

    def ready(*wanted):
        for name in wanted:
            loads[name].wait()

    ready("routes")
    route = r["routes"][...]
    expert = lax.broadcasted_iota(jnp.int32, (devices, row_count), 0)
    onehot = (expert == route).astype(jnp.float32)
    before_row = lax.broadcasted_iota(jnp.int32, (row_count, row_count), 0)
    this_row = lax.broadcasted_iota(jnp.int32, (row_count, row_count), 1)
    earlier = (before_row < this_row).astype(jnp.bfloat16)
    before = jnp.dot(onehot.astype(jnp.bfloat16), earlier, preferred_element_type=jnp.float32)
    rank = jnp.sum(before * onehot, axis=0, keepdims=True).astype(jnp.int32)
    position = route * slot_cap + rank

    sends = [None] * devices

    def pack(start):
        count = min(per_chunk, devices - start)
        amount = count * slot_cap
        line = lax.broadcasted_iota(jnp.int32, (amount, 1), 0)
        wanted = lax.rem(line, slot_cap)
        for number in range(count):
            low = number * slot_cap
            inside = (line >= low) & (line < low + slot_cap)
            wanted = wanted + jnp.where(inside, index_of(order[start + number]) * slot_cap, 0)
        chosen = (wanted == position).astype(jnp.float32)
        used = jnp.sum(chosen, axis=1, keepdims=True) > 0.5
        chosen = chosen.astype(jnp.bfloat16)
        r["select"][pl.ds(start * slot_cap, amount)] = chosen
        rows = jnp.dot(chosen, r["x"][...], preferred_element_type=jnp.float32)
        rows = jnp.where(used, rows, EMPTY).astype(jnp.bfloat16)
        rows = rows.reshape(count, slot_cap, features)
        r["packed"][pl.ds(start, count)] = rows
        if start == 0:
            r["arrived"][0] = rows[0]

    def send(start):
        for place in range(start, min(start + per_chunk, devices)):
            if order[place] == 0:
                continue
            sends[place] = pltpu.make_async_remote_copy(
                src_ref=r["packed"].at[place],
                dst_ref=r["arrived"].at[place],
                send_sem=r["send_sem"].at[place],
                recv_sem=r["recv_sem"].at[place],
                device_id=partner_of(order[place], members),
                device_id_type=MESH,
            )
            sends[place].start()

    ready("x")
    near_chunks = [start for start in chunk_starts if start < devices // 2]
    far_chunks = [start for start in chunk_starts if start >= devices // 2]
    pack_order = []
    for place in range(max(len(near_chunks), len(far_chunks))):
        pack_order += far_chunks[place : place + 1] + near_chunks[place : place + 1]
    pack(pack_order[0])
    pl.semaphore_wait(barrier, devices - 1)
    for start, following in zip(pack_order, pack_order[1:] + [None], strict=True):
        send(start)
        if following is not None:
            pack(following)

    ready("centre", "router", "bias", "encoder", "decoder")
    centre = r["centre"][...].reshape(1, features)
    router = r["router"][...].astype(jnp.float32)
    bias = r["bias"][...]
    error_sum = jnp.zeros((1, features), jnp.float32)
    router_grad = jnp.zeros((1, features), jnp.float32)
    bias_grad = jnp.zeros((1, latent_count), jnp.float32)
    backs = [None] * devices
    for start in chunk_starts:
        places = range(start, min(start + per_chunk, devices))
        for place in places:
            if sends[place] is not None:
                sends[place].wait_recv()
        amount = len(places) * slot_cap
        chunk = pl.ds(start * slot_cap, amount)
        wide = (
            r["arrived"][pl.ds(start, len(places))].reshape(amount, features).astype(jnp.float32)
        )
        live = (wide[:, :1] < 0.5 * EMPTY).astype(jnp.float32)
        gating = jax.nn.sigmoid(jnp.sum(wide * router, axis=1, keepdims=True))
        centred = (wide - centre).astype(jnp.bfloat16)
        preact = jnp.dot(centred, r["encoder"][...], preferred_element_type=jnp.float32) + bias
        positive = jnp.maximum(preact, 0.0)
        latents = (positive * positive).astype(jnp.bfloat16)
        ungated = jnp.dot(latents, r["decoder"][...], preferred_element_type=jnp.float32)
        rebuilt = centre + gating * ungated
        r["outgoing"][pl.ds(start, len(places))] = rebuilt.astype(jnp.bfloat16).reshape(
            len(places), slot_cap, features
        )
        for place in places:
            if order[place] == 0:
                r["returned"][place] = r["outgoing"][place]
                continue
            backs[place] = pltpu.make_async_remote_copy(
                src_ref=r["outgoing"].at[place],
                dst_ref=r["returned"].at[place],
                send_sem=r["back_send"].at[place],
                recv_sem=r["back_recv"].at[place],
                device_id=partner_of(order[place], members),
                device_id_type=MESH,
            )
            if place < devices - HELD_BLOCKS:
                backs[place].start()
        errors = (wide - rebuilt) * live
        backward = (-gating * errors).astype(jnp.bfloat16)
        latent_grad = (
            lax.dot_general(
                backward,
                r["decoder"][...],
                (((1,), (1,)), ((), ())),
                preferred_element_type=jnp.float32,
            )
            + sparsity
        )
        preact_grad = (latent_grad * 2.0 * positive * live).astype(jnp.bfloat16)
        logit_grad = -jnp.sum(errors * ungated, axis=1, keepdims=True) * gating * (1.0 - gating)
        logit_grad = logit_grad.astype(jnp.bfloat16).astype(jnp.float32)
        error_sum = error_sum + jnp.sum(errors, axis=0, keepdims=True)
        router_grad = router_grad + jnp.sum(logit_grad * wide, axis=0, keepdims=True)
        bias_grad = bias_grad + jnp.sum(preact_grad.astype(jnp.float32), axis=0, keepdims=True)
        r["centred_buf"][chunk] = centred
        r["latents_buf"][chunk] = latents
        r["backward_buf"][chunk] = backward
        r["preact_buf"][chunk] = preact_grad

    products = lax.dot_general(
        three_parts(bias_grad),
        r["encoder"][...],
        (((1,), (1,)), ((), ())),
        preferred_element_type=jnp.float32,
    )
    r["part_buf"][0] = -error_sum - jnp.sum(products, axis=0, keepdims=True)
    half_members = members // 2
    my_group, my_member = lax.axis_index("group"), lax.axis_index("member")
    my_place = my_group * half_members + lax.rem(my_member, half_members)
    near = [offset for offset in order if not offset & half_members]
    parts = [None] * len(near)
    for number, offset in enumerate(near):
        if offset:
            parts[number] = pltpu.make_async_remote_copy(
                src_ref=r["part_buf"].at[0],
                dst_ref=r["part_in"].at[my_place],
                send_sem=r["part_send"].at[number],
                recv_sem=r["part_recv"].at[number],
                device_id=partner_of(offset, members),
                device_id_type=MESH,
            )
            parts[number].start()
    r["part_in"][my_place] = r["part_buf"][0]

    def near_sum():
        for copy in parts:
            if copy is not None:
                copy.wait_recv()
        r["part_buf"][1] = jnp.sum(r["part_in"][...], axis=0)
        mirror = pltpu.make_async_remote_copy(
            src_ref=r["part_buf"].at[1],
            dst_ref=r["part_buf"].at[2],
            send_sem=r["part_send"].at[0],
            recv_sem=r["part_recv"].at[0],
            device_id=partner_of(half_members, members),
            device_id_type=MESH,
        )
        mirror.start()
        for place in range(devices - HELD_BLOCKS, devices):
            backs[place].start()
        return mirror

    def recon_part(start, count, first, last):
        for place in range(start, start + count):
            if backs[place] is not None:
                backs[place].wait_recv()
        amount = count * slot_cap
        part = lax.dot_general(
            r["select"][pl.ds(start * slot_cap, amount)],
            r["returned"][pl.ds(start, count)].reshape(amount, features),
            (((0,), (0,)), ((), ())),
            preferred_element_type=jnp.float32,
        )
        total = part if first else r["recon_acc"][...] + part
        if last:
            r["o_recon"][...] = total.astype(jnp.bfloat16)
        else:
            r["recon_acc"][...] = total

    def adam_rows(index, left, right, weights, first, second, outs):
        lanes = pl.ds(pl.multiple_of(index * 128, 128), 128)
        gradient = lax.dot_general(
            left[:, lanes], right[...], (((0,), (0,)), ((), ())), preferred_element_type=jnp.float32
        )
        stepped, first_new, second_new = adam_step(
            weights[lanes], gradient, first[lanes], second[lanes]
        )
        outs[0][lanes] = stepped.astype(outs[0].dtype)
        outs[1][lanes] = first_new
        outs[2][lanes] = second_new

    def decoder_rows(index, carry):
        adam_rows(
            index,
            r["latents_buf"],
            r["backward_buf"],
            r["decoder"],
            r["dm"],
            r["dv"],
            (r["o_decoder"], r["o_decoder_m"], r["o_decoder_v"]),
        )
        return carry

    def encoder_rows(index, carry):
        adam_rows(
            index,
            r["centred_buf"],
            r["preact_buf"],
            r["encoder"],
            r["em"],
            r["ev"],
            (r["o_encoder"], r["o_encoder_m"], r["o_encoder_v"]),
        )
        return carry

    half = devices // 2
    recon_part(0, half, True, False)
    mirror = near_sum()
    ready("dm", "dv")
    lax.fori_loop(0, latent_count // 128, decoder_rows, 0)
    ready("em", "ev", "router_m", "router_v", "bias_m", "bias_v", "centre_m", "centre_v")
    lax.fori_loop(0, features // 128, encoder_rows, 0)
    for kind, gradient in (("router", router_grad), ("bias", bias_grad)):
        stepped, first_new, second_new = adam_step(
            r[kind][...], gradient, r[kind + "_m"][...], r[kind + "_v"][...]
        )
        r["o_" + kind][...] = stepped.astype(r["o_" + kind].dtype)
        r["o_" + kind + "_m"][...] = first_new
        r["o_" + kind + "_v"][...] = second_new
    mirror.wait_recv()
    stepped, first_new, second_new = adam_step(
        centre,
        r["part_buf"][1] + r["part_buf"][2],
        r["centre_m"][...].reshape(1, features),
        r["centre_v"][...].reshape(1, features),
    )
    r["o_centre"][...] = stepped.reshape(features)
    r["o_centre_m"][...] = first_new.reshape(features)
    r["o_centre_v"][...] = second_new.reshape(features)
    left = [start for start in chunk_starts if start >= half]
    for start in left:
        recon_part(start, min(per_chunk, devices - start), False, start == left[-1])
    for copy in sends + backs + parts + [mirror]:
        if copy is not None:
            copy.wait_send()


def write_kernel(count, *refs):
    sems = refs[-1]
    copies = []
    for number in range(count):
        copies.append(
            pltpu.make_async_copy(refs[number], refs[count + number], sems.at[number])
        )
        copies[-1].start()
    for copy in copies:
        copy.wait()


def whole_step(rows, routes, operands, members, devices):
    row_count, features = rows.shape
    encoder = operands[6]
    latent_count = encoder.shape[1]
    slot_cap = 2 * row_count // devices
    slots = devices * slot_cap
    inputs = tuple(
        pltpu.with_memory_space_constraint(value, pltpu.HBM)
        for value in (rows, routes.reshape(1, row_count), *operands)
    )
    in_vmem = pl.BlockSpec(memory_space=pltpu.VMEM)
    in_hbm = pl.BlockSpec(memory_space=pltpu.HBM)
    anywhere = pl.BlockSpec(memory_space=pl.ANY)
    bf16, f32 = jnp.bfloat16, jnp.float32
    by_feature, by_latent = (features, latent_count), (latent_count, features)
    outs = [
        ((row_count, features), bf16),
        ((features,), f32),
        ((features,), f32),
        ((features,), f32),
        ((1, features), bf16),
        ((1, features), f32),
        ((1, features), f32),
        (by_feature, bf16),
        ((1, latent_count), f32),
        (by_latent, bf16),
        (by_feature, f32),
        (by_feature, f32),
        ((1, latent_count), f32),
        ((1, latent_count), f32),
        (by_latent, f32),
        (by_latent, f32),
    ]
    out_shape = tuple(jax.ShapeDtypeStruct(shape, dtype) for shape, dtype in outs)
    blocks = (devices, slot_cap, features)
    results = pl.pallas_call(
        functools.partial(whole_kernel, devices, members, slot_cap),
        out_shape=out_shape,
        in_specs=[in_hbm] * len(inputs),
        out_specs=(in_vmem,) * len(outs),
        scratch_shapes=[
            *(pltpu.VMEM(value.shape, value.dtype) for value in inputs),
            pltpu.VMEM((slots, row_count), bf16),
            pltpu.VMEM(blocks, bf16),
            pltpu.VMEM(blocks, bf16),
            pltpu.VMEM(blocks, bf16),
            pltpu.VMEM(blocks, bf16),
            pltpu.VMEM((slots, features), bf16),
            pltpu.VMEM((slots, latent_count), bf16),
            pltpu.VMEM((slots, features), bf16),
            pltpu.VMEM((slots, latent_count), bf16),
            pltpu.VMEM((row_count, features), f32),
            pltpu.VMEM((3, 1, features), f32),
            pltpu.VMEM((devices // 2, 1, features), f32),
            pltpu.SemaphoreType.DMA((len(inputs),)),
            pltpu.SemaphoreType.DMA((devices,)),
            pltpu.SemaphoreType.DMA((devices,)),
            pltpu.SemaphoreType.DMA((devices,)),
            pltpu.SemaphoreType.DMA((devices,)),
            pltpu.SemaphoreType.DMA((devices // 2,)),
            pltpu.SemaphoreType.DMA((devices // 2,)),
        ],
        compiler_params=pltpu.CompilerParams(
            collective_id=0, has_side_effects=True, vmem_limit_bytes=VMEM_LIMIT
        ),
        name="whole_step",
    )(*inputs)
    return pl.pallas_call(
        functools.partial(write_kernel, len(outs)),
        out_shape=out_shape,
        in_specs=[in_vmem] * len(outs),
        out_specs=(anywhere,) * len(outs),
        scratch_shapes=[pltpu.SemaphoreType.DMA((len(outs),))],
        compiler_params=pltpu.CompilerParams(vmem_limit_bytes=1 << 20),
        name="write_results",
    )(*results)


def three_parts(values):
    high = values.astype(jnp.bfloat16).astype(jnp.float32)
    middle = (values - high).astype(jnp.bfloat16).astype(jnp.float32)
    low = values - high - middle
    row = lax.broadcasted_iota(jnp.int32, (16, values.shape[1]), 0)
    stacked = jnp.where(
        row == 0, high, jnp.where(row == 1, middle, jnp.where(row == 2, low, 0.0))
    )
    return stacked.astype(jnp.bfloat16)


def centre_kernel(devices, members, part_ref, total_ref, parts, send_sem, recv_sem):
    greet(devices, members)
    copies = []
    for offset in range(1, devices):
        copies.append(
            pltpu.make_async_remote_copy(
                src_ref=part_ref,
                dst_ref=parts.at[lax.axis_index("group") * members + lax.axis_index("member")],
                send_sem=send_sem.at[offset],
                recv_sem=recv_sem.at[offset],
                device_id=partner_of(offset, members),
                device_id_type=MESH,
            )
        )
        copies[-1].start()
    parts[lax.axis_index("group") * members + lax.axis_index("member")] = part_ref[...]
    for copy in copies:
        copy.wait_recv()
    total_ref[...] = jnp.sum(parts[...], axis=0)
    for copy in copies:
        copy.wait_send()


def centre_sum(part, devices, members):
    shape = (1, part.shape[0])
    return pl.pallas_call(
        functools.partial(centre_kernel, devices, members),
        out_shape=jax.ShapeDtypeStruct(shape, jnp.float32),
        in_specs=[pl.BlockSpec(memory_space=pltpu.VMEM)],
        out_specs=pl.BlockSpec(memory_space=pltpu.VMEM),
        scratch_shapes=[
            pltpu.VMEM((devices,) + shape, jnp.float32),
            pltpu.SemaphoreType.DMA((devices,)),
            pltpu.SemaphoreType.DMA((devices,)),
        ],
        compiler_params=pltpu.CompilerParams(
            collective_id=1, has_side_effects=True, vmem_limit_bytes=4 << 20
        ),
        name="centre_sum",
    )(part[None])[0]


def power_of_two(number):
    return number & (number - 1) == 0


def power_of_two(number):
    return number & (number - 1) == 0


def per_device(
    activations,
    routes,
    centre_bias,
    centre_first,
    centre_second,
    router,
    router_first,
    router_second,
    encoder,
    enc_bias,
    decoder,
    encoder_first,
    encoder_second,
    enc_bias_first,
    enc_bias_second,
    decoder_first,
    decoder_second,
):
    groups = lax.axis_size("group")
    members = lax.axis_size("member")
    devices = groups * members
    row_count = activations.shape[0]
    feature_count = activations.shape[1]
    slot_cap = 2 * row_count // devices
    aligned = slot_cap % 16 == 0 and power_of_two(groups) and power_of_two(members)
    aligned = aligned and members > 1 and row_count % 128 == 0
    aligned = aligned and feature_count % 128 == 0 and enc_bias.shape[1] % 128 == 0
    if aligned:
        operands = (
            centre_bias,
            centre_first,
            centre_second,
            router,
            router_first,
            router_second,
            encoder[0],
            enc_bias,
            decoder[0],
            encoder_first[0],
            encoder_second[0],
            enc_bias_first,
            enc_bias_second,
            decoder_first[0],
            decoder_second[0],
        )
        results = list(whole_step(activations, routes, operands, members, devices))
        for number in (7, 9, 10, 11, 14, 15):
            results[number] = results[number][None]
        return tuple(results)
    route_ids = routes[:, 0]
    onehot = (route_ids[:, None] == jnp.arange(devices, dtype=jnp.int32)[None, :]).astype(
        jnp.bfloat16
    )
    earlier = (jnp.arange(row_count)[:, None] > jnp.arange(row_count)[None, :]).astype(jnp.bfloat16)
    before = jnp.dot(earlier, onehot, preferred_element_type=jnp.float32)
    slot_rank = jnp.sum(before * onehot.astype(jnp.float32), axis=1).astype(jnp.int32)
    position = route_ids * slot_cap + slot_rank
    chosen = jnp.arange(devices * slot_cap, dtype=jnp.int32)[:, None] == position[None, :]
    select = chosen.astype(jnp.bfloat16)
    used = jnp.any(chosen, axis=1)
    packed = jnp.where(
        used[:, None],
        jnp.dot(select, activations, preferred_element_type=jnp.float32),
        EMPTY,
    ).astype(jnp.bfloat16)
    packed = packed.reshape(devices, slot_cap, feature_count)
    arrived = lax.all_to_all(
        packed, ("group", "member"), split_axis=0, concat_axis=0, tiled=True
    )
    in_rows = arrived.reshape(devices * slot_cap, feature_count)
    live_mask = (in_rows[:, 0] < 0.5 * EMPTY).astype(jnp.float32)
    centred, positive, latents, gating, ungated, rebuilt = forward_pass(
        in_rows, centre_bias, router[0], encoder[0], enc_bias[0], decoder[0]
    )
    outgoing = rebuilt.astype(jnp.bfloat16)
    returned = lax.all_to_all(
        outgoing.reshape(devices, slot_cap, feature_count),
        ("group", "member"),
        split_axis=0,
        concat_axis=0,
        tiled=True,
    )
    recon = lax.dot_general(
        select,
        returned.reshape(devices * slot_cap, feature_count),
        (((0,), (0,)), ((), ())),
        preferred_element_type=jnp.float32,
    ).astype(jnp.bfloat16)
    encoder_grad, bias_grad, decoder_grad, router_grad, centre_part = backward_pass(
        in_rows,
        live_mask,
        centred,
        positive,
        latents,
        gating,
        ungated,
        rebuilt,
        encoder[0],
        decoder[0],
    )
    router_new = adam_update(router[0], router_grad, router_first[0], router_second[0])
    encoder_new = adam_update(encoder[0], encoder_grad, encoder_first[0], encoder_second[0])
    bias_new = adam_update(enc_bias[0], bias_grad, enc_bias_first[0], enc_bias_second[0])
    decoder_new = adam_update(decoder[0], decoder_grad, decoder_first[0], decoder_second[0])
    if power_of_two(groups) and power_of_two(members):
        centre_part, first, second = lax.optimization_barrier(
            (centre_part, encoder_new[1], decoder_new[1])
        )
        encoder_new = (encoder_new[0], first, encoder_new[2])
        decoder_new = (decoder_new[0], second, decoder_new[2])
        centre_total = centre_sum(centre_part, devices, members)
    else:
        centre_total = lax.psum(centre_part, ("group", "member"))
    centre_new = adam_update(centre_bias, centre_total, centre_first, centre_second)
    return (
        recon,
        centre_new[0],
        centre_new[1],
        centre_new[2],
        router_new[0][None],
        router_new[1][None],
        router_new[2][None],
        encoder_new[0][None],
        bias_new[0][None],
        decoder_new[0][None],
        encoder_new[1][None],
        encoder_new[2][None],
        bias_new[1][None],
        bias_new[2][None],
        decoder_new[1][None],
        decoder_new[2][None],
    )


def solution(mesh):
    placed = (
        P(("group", "member"), None),
        P(("group", "member"), None),
        P(),
        P(),
        P(),
        P(("group", "member"), None),
        P(("group", "member"), None),
        P(("group", "member"), None),
        P(("group", "member"), None, None),
        P(("group", "member"), None),
        P(("group", "member"), None, None),
        P(("group", "member"), None, None),
        P(("group", "member"), None, None),
        P(("group", "member"), None),
        P(("group", "member"), None),
        P(("group", "member"), None, None),
        P(("group", "member"), None, None),
    )
    return jax.shard_map(
        per_device,
        mesh=mesh,
        in_specs=placed,
        out_specs=(
            P(("group", "member"), None),
            P(),
            P(),
            P(),
            P(("group", "member"), None),
            P(("group", "member"), None),
            P(("group", "member"), None),
            P(("group", "member"), None, None),
            P(("group", "member"), None),
            P(("group", "member"), None, None),
            P(("group", "member"), None, None),
            P(("group", "member"), None, None),
            P(("group", "member"), None),
            P(("group", "member"), None),
            P(("group", "member"), None, None),
            P(("group", "member"), None, None),
        ),
        check_vma=False,
    )
```

```python
import functools
import types

import jax
import jax.numpy as jnp
from jax import lax
from jax.experimental import pallas as pl
from jax.experimental.pallas import tpu as pltpu
from jax.sharding import PartitionSpec as P

MESH = pl.DeviceIdType.MESH
AXES = ("group", "member")

STEP = 10


learn_rate = 0.001
beta_one = 0.9
beta_two = 0.999
adam_eps = 1e-08
sparsity = 0.1
EMPTY = 16.0
VMEM_LIMIT = 40 << 20
HELD_BLOCKS = 8
EARLY_NEAR = 2


def adam_update(weights_in, gradient, moment_one, moment_two):
    first_new = beta_one * moment_one + (1.0 - beta_one) * gradient
    second_new = beta_two * moment_two + (1.0 - beta_two) * gradient * gradient
    first_hat = first_new / (1.0 - beta_one**STEP)
    second_hat = second_new / (1.0 - beta_two**STEP)
    stepped = weights_in.astype(jnp.float32) - learn_rate * first_hat / (
        jnp.sqrt(second_hat) + adam_eps
    )
    return (stepped.astype(weights_in.dtype), first_new, second_new)


def forward_pass(in_rows, centre_bias, router_row, encoder, enc_bias, decoder):
    centred = (in_rows.astype(jnp.float32) - centre_bias).astype(jnp.bfloat16)
    preact = jnp.dot(centred, encoder, preferred_element_type=jnp.float32) + enc_bias
    positive = jnp.maximum(preact, 0.0)
    latents = (positive * positive).astype(jnp.bfloat16)
    router_wide = jnp.broadcast_to(router_row[:, None], (router_row.shape[0], 128))
    logits = jnp.dot(in_rows, router_wide, preferred_element_type=jnp.float32)[:, 0]
    gating = jax.nn.sigmoid(logits)
    ungated = jnp.dot(latents, decoder, preferred_element_type=jnp.float32)
    rebuilt = centre_bias + gating[:, None] * ungated
    return (centred, positive, latents, gating, ungated, rebuilt)


def backward_pass(
    in_rows, live_mask, centred, positive, latents, gating, ungated, rebuilt, encoder, decoder
):
    errors = (in_rows.astype(jnp.float32) - rebuilt) * live_mask[:, None]
    backward = (-gating[:, None] * errors).astype(jnp.bfloat16)
    decoder_grad = jnp.dot(latents.T, backward, preferred_element_type=jnp.float32)
    latent_grad = jnp.dot(backward, decoder.T, preferred_element_type=jnp.float32) + sparsity
    preact_grad = (latent_grad * 2.0 * positive * live_mask[:, None]).astype(jnp.bfloat16)
    encoder_grad = jnp.dot(centred.T, preact_grad, preferred_element_type=jnp.float32)
    bias_grad = jnp.sum(preact_grad.astype(jnp.float32), axis=0)
    logit_grad = (-jnp.sum(errors * ungated, axis=1) * gating * (1.0 - gating)).astype(jnp.bfloat16)
    router_grad = jnp.dot(logit_grad, in_rows, preferred_element_type=jnp.float32)
    centre_part = -jnp.sum(errors, axis=0) - jnp.dot(
        encoder.astype(jnp.float32), bias_grad, precision=lax.Precision.HIGHEST
    )
    return (encoder_grad, bias_grad, decoder_grad, router_grad, centre_part)


def flipped(index, bits):
    result, place = index, 1
    while place <= bits:
        if bits & place:
            result = result + (1 - 2 * lax.rem(lax.div(index, place), 2)) * place
        place *= 2
    return result


def partner_of(offset, members):
    return (
        flipped(lax.axis_index("group"), offset // members),
        flipped(lax.axis_index("member"), offset % members),
    )


def greet(devices, members):
    barrier = pltpu.get_barrier_semaphore()
    for offset in range(1, devices):
        pl.semaphore_signal(
            barrier, inc=1, device_id=partner_of(offset, members), device_id_type=MESH
        )
    pl.semaphore_wait(barrier, devices - 1)


IN_NAMES = (
    "x",
    "routes",
    "centre",
    "centre_m",
    "centre_v",
    "router",
    "router_m",
    "router_v",
    "encoder",
    "bias",
    "decoder",
    "em",
    "ev",
    "bias_m",
    "bias_v",
    "dm",
    "dv",
)
OUT_NAMES = (
    "o_recon",
    "o_centre",
    "o_centre_m",
    "o_centre_v",
    "o_router",
    "o_router_m",
    "o_router_v",
    "o_encoder",
    "o_bias",
    "o_decoder",
    "o_encoder_m",
    "o_encoder_v",
    "o_bias_m",
    "o_bias_v",
    "o_decoder_m",
    "o_decoder_v",
    "o_flag",
)
SCRATCH_NAMES = (
    "near_sel",
    "far_sel",
    "over_sel",
    "near_out",
    "far_out",
    "over_out",
    "meta_out",
    "near_in",
    "far_in",
    "over_in",
    "meta_in",
    "relay_out",
    "relay_in",
    "near_back",
    "far_back",
    "over_back",
    "near_ret",
    "far_ret",
    "relay_back",
    "comp_out",
    "comp_in",
    "match",
    "centred_buf",
    "latents_buf",
    "backward_buf",
    "preact_buf",
    "recon_acc",
    "part_buf",
    "part_in",
    "local_sem",
    "near_send",
    "near_recv",
    "far_send",
    "far_recv",
    "relay_send",
    "relay_recv",
    "nback_send",
    "nback_recv",
    "fback_send",
    "fback_recv",
    "rback_send",
    "rback_recv",
    "over_send",
    "over_recv",
    "part_send",
    "part_recv",
)
REF_NAMES = (
    tuple(name + "_in" for name in IN_NAMES)
    + OUT_NAMES
    + IN_NAMES
    + SCRATCH_NAMES
)
LOAD_ORDER = (
    "routes",
    "x",
    "encoder",
    "decoder",
    "centre",
    "router",
    "bias",
    "dm",
    "dv",
    "em",
    "ev",
    "router_m",
    "router_v",
    "bias_m",
    "bias_v",
    "centre_m",
    "centre_v",
)


def adam_step(weights, gradient, moment_one, moment_two):
    first_new = beta_one * moment_one + (1.0 - beta_one) * gradient
    second_new = beta_two * moment_two + (1.0 - beta_two) * (gradient * gradient)
    scaled = first_new * (learn_rate / (1.0 - beta_one**STEP))
    root = jnp.sqrt(second_new * (1.0 / (1.0 - beta_two**STEP))) + adam_eps
    return (weights.astype(jnp.float32) - scaled / root, first_new, second_new)


def lane_count(values, weights):
    tall = jnp.broadcast_to(values, (16, values.shape[1])).astype(jnp.bfloat16)
    return jnp.dot(tall, weights, preferred_element_type=jnp.float32)[:1]


def picked(wanted, positions):
    line = lax.broadcasted_iota(jnp.int32, (wanted, 1), 0)
    return (line == positions).astype(jnp.float32)


def unpick(chosen, rows):
    return lax.dot_general(
        chosen, rows, (((0,), (0,)), ((), ())), preferred_element_type=jnp.float32
    )


def whole_kernel(devices, members, slot_cap, *refs):
    r = types.SimpleNamespace(**dict(zip(REF_NAMES, refs, strict=True)))
    half_members = members // 2
    half = devices // 2
    base = slot_cap // 2
    near = [offset for offset in range(devices) if not offset & half_members]
    per_chunk = min(half, max(1, 128 // slot_cap))
    starts = list(range(0, half, per_chunk))
    row_count, features = r.x.shape
    latent_count = r.bias.shape[1]
    over_cap = r.over_sel.shape[0]
    my_group, my_member = lax.axis_index("group"), lax.axis_index("member")
    me = my_group * members + my_member

    barrier = pltpu.get_barrier_semaphore()
    for offset in range(1, devices):
        pl.semaphore_signal(
            barrier, inc=1, device_id=partner_of(offset, members), device_id_type=MESH
        )
    loads = {}
    for number, name in enumerate(LOAD_ORDER):
        loads[name] = pltpu.make_async_copy(
            getattr(r, name + "_in"), getattr(r, name), r.local_sem.at[number]
        )
        loads[name].start()

    def ready(*wanted):
        for name in wanted:
            loads[name].wait()

    def remote(source, target, send_sem, recv_sem, offset):
        copy = pltpu.make_async_remote_copy(
            src_ref=source,
            dst_ref=target,
            send_sem=send_sem,
            recv_sem=recv_sem,
            device_id=partner_of(offset, members),
            device_id_type=MESH,
        )
        sent.append(copy)
        return copy

    sent = []

    ready("routes")
    route = r.routes[...]
    expert = lax.broadcasted_iota(jnp.int32, (devices, row_count), 0)
    onehot = (expert == route).astype(jnp.float32)
    before_row = lax.broadcasted_iota(jnp.int32, (row_count, row_count), 0)
    this_row = lax.broadcasted_iota(jnp.int32, (row_count, row_count), 1)
    earlier = (before_row < this_row).astype(jnp.bfloat16)
    before = jnp.dot(onehot.astype(jnp.bfloat16), earlier, preferred_element_type=jnp.float32)
    rank = jnp.sum(before * onehot, axis=0, keepdims=True).astype(jnp.int32)
    apart = lax.bitwise_xor(route, jnp.broadcast_to(me, route.shape))
    inner = lax.bitwise_and(apart, members - 1)
    outer = lax.shift_right_logical(apart, members.bit_length() - 1)
    is_far = inner >= half_members
    place = outer * half_members + lax.bitwise_and(inner, half_members - 1)
    is_over = is_far & (rank >= base)
    over_line = is_over.astype(jnp.float32)
    over_rank = lane_count(over_line, earlier).astype(jnp.int32)
    over_total = jnp.sum(over_line, axis=1, keepdims=True)
    flag = (over_total > over_cap).astype(jnp.float32)
    near_at = jnp.where(is_far, -1, place * slot_cap + rank)
    far_at = jnp.where(is_far & (rank < base), place * base + rank, -1)
    over_at = jnp.where(is_over, over_rank, -1)
    over_slot = jnp.where(is_over, place * base + rank - (base - 1), 0).astype(jnp.float32)

    ready("x")

    def packed(chosen, bottom):
        rows = jnp.dot(chosen.astype(jnp.bfloat16), r.x[...], preferred_element_type=jnp.float32)
        if bottom is None:
            return rows
        used = jnp.sum(chosen, axis=1, keepdims=True) > 0.5
        return jnp.where(used, rows, bottom)

    chosen = picked(over_cap, over_at)
    r.over_sel[...] = chosen.astype(jnp.bfloat16)
    r.over_out[...] = packed(chosen, None).astype(jnp.bfloat16)
    tall_slot = jnp.broadcast_to(over_slot, (16, row_count)).astype(jnp.bfloat16)
    r.meta_out[...] = lax.dot_general(
        tall_slot,
        r.over_sel[...],
        (((1,), (1,)), ((), ())),
        preferred_element_type=jnp.float32,
    )
    pl.semaphore_wait(barrier, devices - 1)
    rows_hop = remote(
        r.over_out, r.over_in, r.over_send.at[0], r.over_recv.at[0], half_members
    )
    meta_hop = remote(
        r.meta_out, r.meta_in, r.over_send.at[1], r.over_recv.at[1], half_members
    )
    meta_hop.start()
    rows_hop.start()

    near_go = [None] * half

    def near_pack(start):
        amount = per_chunk * slot_cap
        chosen = picked(amount, near_at - start * slot_cap)
        r.near_sel[pl.ds(start * slot_cap, amount)] = chosen.astype(jnp.bfloat16)
        rows = packed(chosen, EMPTY).reshape(per_chunk, slot_cap, features).astype(jnp.bfloat16)
        r.near_out[pl.ds(start, per_chunk)] = rows
        for number in range(start, start + per_chunk):
            if near[number] == 0:
                r.near_in[number] = rows[number - start]
                continue
            near_go[number] = remote(
                r.near_out.at[number],
                r.near_in.at[number],
                r.near_send.at[number],
                r.near_recv.at[number],
                near[number],
            )
            near_go[number].start()

    for start in starts[:EARLY_NEAR]:
        near_pack(start)

    chosen = picked(half * base, far_at)
    r.far_sel[...] = chosen.astype(jnp.bfloat16)
    r.far_out[...] = packed(chosen, EMPTY).reshape(half, base, features).astype(jnp.bfloat16)
    far_go = []
    for number, offset in enumerate(near):
        far_go.append(
            remote(
                r.far_out.at[number],
                r.far_in.at[number],
                r.far_send.at[number],
                r.far_recv.at[number],
                offset + half_members,
            )
        )
        far_go[-1].start()

    meta_hop.wait_recv()
    line = lax.broadcasted_iota(jnp.int32, (half * base, 1), 0).astype(jnp.float32)
    match = (line + 1.0 == r.meta_in[pl.ds(0, 1)]).astype(jnp.float32)
    taken = jnp.sum(match, axis=1, keepdims=True) > 0.5
    r.match[...] = match.astype(jnp.bfloat16)
    rows_hop.wait_recv()
    rows = jnp.dot(r.match[...], r.over_in[...], preferred_element_type=jnp.float32)
    rows = jnp.where(taken, rows, EMPTY).reshape(half, base, features).astype(jnp.bfloat16)
    r.relay_out[...] = rows
    relay_go = [None] * half
    for number, offset in enumerate(near):
        if offset == 0:
            r.relay_in[number] = rows[number]
            continue
        relay_go[number] = remote(
            r.relay_out.at[number],
            r.relay_in.at[number],
            r.relay_send.at[number],
            r.relay_recv.at[number],
            offset,
        )
        relay_go[number].start()
    for start in starts[EARLY_NEAR:]:
        near_pack(start)

    ready("centre", "router", "bias", "encoder", "decoder")
    centre = r.centre[...].reshape(1, features)
    router = r.router[...].astype(jnp.float32)
    bias = r.bias[...]
    sums = [
        jnp.zeros((1, features), jnp.float32),
        jnp.zeros((1, features), jnp.float32),
        jnp.zeros((1, latent_count), jnp.float32),
    ]

    def compute(wide, line, send_back):
        amount = wide.shape[0]
        live = (wide[:, :1] < 0.5 * EMPTY).astype(jnp.float32)
        gating = jax.nn.sigmoid(jnp.sum(wide * router, axis=1, keepdims=True))
        centred = (wide - centre).astype(jnp.bfloat16)
        preact = jnp.dot(centred, r.encoder[...], preferred_element_type=jnp.float32) + bias
        positive = jnp.maximum(preact, 0.0)
        latents = (positive * positive).astype(jnp.bfloat16)
        ungated = jnp.dot(latents, r.decoder[...], preferred_element_type=jnp.float32)
        rebuilt = centre + gating * ungated
        send_back(rebuilt)
        errors = (wide - rebuilt) * live
        backward = (-gating * errors).astype(jnp.bfloat16)
        latent_grad = (
            lax.dot_general(
                backward,
                r.decoder[...],
                (((1,), (1,)), ((), ())),
                preferred_element_type=jnp.float32,
            )
            + sparsity
        )
        preact_grad = (latent_grad * 2.0 * positive * live).astype(jnp.bfloat16)
        logit_grad = -jnp.sum(errors * ungated, axis=1, keepdims=True) * gating * (1.0 - gating)
        logit_grad = logit_grad.astype(jnp.bfloat16).astype(jnp.float32)
        sums[0] = sums[0] + jnp.sum(errors, axis=0, keepdims=True)
        sums[1] = sums[1] + jnp.sum(logit_grad * wide, axis=0, keepdims=True)
        sums[2] = sums[2] + jnp.sum(preact_grad.astype(jnp.float32), axis=0, keepdims=True)
        chunk = pl.ds(line, amount)
        r.centred_buf[chunk] = centred
        r.latents_buf[chunk] = latents
        r.backward_buf[chunk] = backward
        r.preact_buf[chunk] = preact_grad

    near_come, far_come, relay_come = [None] * half, [None] * half, [None] * half

    def near_chunk(start):
        numbers = range(start, start + per_chunk)
        for number in numbers:
            if near_go[number] is not None:
                near_go[number].wait_recv()
        wide = r.near_in[pl.ds(start, per_chunk)].reshape(per_chunk * slot_cap, features)

        def send_back(rebuilt):
            r.near_back[pl.ds(start, per_chunk)] = rebuilt.astype(jnp.bfloat16).reshape(
                per_chunk, slot_cap, features
            )
            for number in numbers:
                if near[number] == 0:
                    r.near_ret[number] = r.near_back[number]
                    continue
                near_come[number] = remote(
                    r.near_back.at[number],
                    r.near_ret.at[number],
                    r.nback_send.at[number],
                    r.nback_recv.at[number],
                    near[number],
                )
                near_come[number].start()

        compute(wide.astype(jnp.float32), start * slot_cap, send_back)

    def passed_chunk():
        for copy in relay_go:
            if copy is not None:
                copy.wait_recv()
        wide = r.relay_in[...].astype(jnp.float32).reshape(half * base, features)

        def send_back(rebuilt):
            r.over_back[...] = rebuilt.reshape(half, base, features).astype(jnp.bfloat16)
            for number, offset in enumerate(near):
                if offset == 0:
                    r.relay_back[number] = r.over_back[number]
                    continue
                relay_come[number] = remote(
                    r.over_back.at[number],
                    r.relay_back.at[number],
                    r.rback_send.at[number],
                    r.rback_recv.at[number],
                    offset,
                )
                relay_come[number].start()

        compute(wide, half * slot_cap, send_back)

    def direct_chunk(start, count):
        numbers = range(start, start + count)
        for number in numbers:
            far_go[number].wait_recv()
        wide = r.far_in[pl.ds(start, count)].astype(jnp.float32).reshape(count * base, features)

        def send_back(rebuilt):
            r.far_back[pl.ds(start, count)] = rebuilt.reshape(count, base, features).astype(
                jnp.bfloat16
            )
            for number in numbers:
                far_come[number] = remote(
                    r.far_back.at[number],
                    r.far_ret.at[number],
                    r.fback_send.at[number],
                    r.fback_recv.at[number],
                    near[number] + half_members,
                )
                if number < half - HELD_BLOCKS:
                    far_come[number].start()

        compute(wide, half * slot_cap + (half + start) * base, send_back)

    def pass_back():
        for copy in relay_come:
            if copy is not None:
                copy.wait_recv()
        back = r.relay_back[...].astype(jnp.float32).reshape(half * base, features)
        back = back.astype(jnp.bfloat16)
        r.comp_out[...] = unpick(r.match[...], back).astype(jnp.bfloat16)
        hop = remote(r.comp_out, r.comp_in, r.over_send.at[2], r.over_recv.at[2], half_members)
        hop.start()
        return hop

    for start in starts:
        near_chunk(start)
    direct_chunk(0, half // 2)
    direct_chunk(half // 2, half // 2)
    passed_chunk()
    for number in range(half - HELD_BLOCKS, half - 4):
        far_come[number].start()
    error_sum, router_grad, bias_grad = sums
    products = lax.dot_general(
        three_parts(bias_grad),
        r.encoder[...],
        (((1,), (1,)), ((), ())),
        preferred_element_type=jnp.float32,
    )
    part = -error_sum - jnp.sum(products, axis=0, keepdims=True)
    part = jnp.concatenate([part, jnp.broadcast_to(flag, (1, 128))], axis=1)
    r.part_buf[0] = part
    my_place = my_group * half_members + lax.rem(my_member, half_members)
    parts = [None] * half
    for number, offset in enumerate(near):
        if offset:
            parts[number] = remote(
                r.part_buf.at[0],
                r.part_in.at[my_place],
                r.part_send.at[number],
                r.part_recv.at[number],
                offset,
            )
            parts[number].start()
    r.part_in[my_place] = part

    def adam_rows(index, left, right, weights, first, second, outs):
        lanes = pl.ds(pl.multiple_of(index * 128, 128), 128)
        gradient = unpick(left[:, lanes], right[...])
        stepped, first_new, second_new = adam_step(
            weights[lanes], gradient, first[lanes], second[lanes]
        )
        outs[0][lanes] = stepped.astype(outs[0].dtype)
        outs[1][lanes] = first_new
        outs[2][lanes] = second_new

    def decoder_rows(index, carry):
        outs = (r.o_decoder, r.o_decoder_m, r.o_decoder_v)
        adam_rows(index, r.latents_buf, r.backward_buf, r.decoder, r.dm, r.dv, outs)
        return carry

    def encoder_rows(index, carry):
        outs = (r.o_encoder, r.o_encoder_m, r.o_encoder_v)
        adam_rows(index, r.centred_buf, r.preact_buf, r.encoder, r.em, r.ev, outs)
        return carry

    for copy in near_come:
        if copy is not None:
            copy.wait_recv()
    r.recon_acc[...] = unpick(
        r.near_sel[...], r.near_ret[...].reshape(half * slot_cap, features)
    )
    for copy in parts:
        if copy is not None:
            copy.wait_recv()
    r.part_buf[1] = jnp.sum(r.part_in[...], axis=0)
    mirror = remote(
        r.part_buf.at[1], r.part_buf.at[2], r.part_send.at[0], r.part_recv.at[0], half_members
    )
    mirror.start()
    for number in range(half - 4, half):
        far_come[number].start()
    comp_hop = pass_back()

    ready("dm", "dv")
    lax.fori_loop(0, latent_count // 128, decoder_rows, 0)
    ready("em", "ev", "router_m", "router_v", "bias_m", "bias_v", "centre_m", "centre_v")
    lax.fori_loop(0, features // 128, encoder_rows, 0)
    stepped, r.o_router_m[...], r.o_router_v[...] = adam_step(
        r.router[...], router_grad, r.router_m[...], r.router_v[...]
    )
    r.o_router[...] = stepped.astype(r.o_router.dtype)
    r.o_bias[...], r.o_bias_m[...], r.o_bias_v[...] = adam_step(
        bias, bias_grad, r.bias_m[...], r.bias_v[...]
    )
    mirror.wait_recv()
    total = r.part_buf[1] + r.part_buf[2]
    r.o_flag[...] = total[:, features:]
    stepped, first_new, second_new = adam_step(
        centre,
        total[:, :features],
        r.centre_m[...].reshape(1, features),
        r.centre_v[...].reshape(1, features),
    )
    r.o_centre[...] = stepped.reshape(features)
    r.o_centre_m[...] = first_new.reshape(features)
    r.o_centre_v[...] = second_new.reshape(features)
    for copy in far_come:
        copy.wait_recv()
    back = r.far_ret[...].astype(jnp.float32).reshape(half * base, features)
    r.recon_acc[...] = r.recon_acc[...] + unpick(r.far_sel[...], back.astype(jnp.bfloat16))
    comp_hop.wait_recv()
    recon = r.recon_acc[...] + unpick(r.over_sel[...], r.comp_in[...])
    r.o_recon[...] = recon.astype(jnp.bfloat16)
    for copy in sent:
        copy.wait_send()


def write_kernel(count, *refs):
    sems = refs[-1]
    copies = []
    for number in range(count):
        copies.append(
            pltpu.make_async_copy(refs[number], refs[count + number], sems.at[number])
        )
        copies[-1].start()
    for copy in copies:
        copy.wait()


def whole_step(rows, routes, operands, members, devices):
    row_count, features = rows.shape
    encoder = operands[6]
    latent_count = encoder.shape[1]
    slot_cap = 2 * row_count // devices
    slots = devices * slot_cap
    inputs = tuple(
        pltpu.with_memory_space_constraint(value, pltpu.HBM)
        for value in (rows, routes.reshape(1, row_count), *operands)
    )
    in_vmem = pl.BlockSpec(memory_space=pltpu.VMEM)
    in_hbm = pl.BlockSpec(memory_space=pltpu.HBM)
    bf16, f32 = jnp.bfloat16, jnp.float32
    by_feature, by_latent = (features, latent_count), (latent_count, features)
    outs = [
        ((row_count, features), bf16),
        ((features,), f32),
        ((features,), f32),
        ((features,), f32),
        ((1, features), bf16),
        ((1, features), f32),
        ((1, features), f32),
        (by_feature, bf16),
        ((1, latent_count), f32),
        (by_latent, bf16),
        (by_feature, f32),
        (by_feature, f32),
        ((1, latent_count), f32),
        ((1, latent_count), f32),
        (by_latent, f32),
        (by_latent, f32),
        ((1, 128), f32),
    ]
    out_shape = tuple(jax.ShapeDtypeStruct(shape, dtype) for shape, dtype in outs)
    half, base = devices // 2, slot_cap // 2
    over_cap = slots // 8
    near_blocks = (half, slot_cap, features)
    far_blocks = (half, base, features)
    results = pl.pallas_call(
        functools.partial(whole_kernel, devices, members, slot_cap),
        out_shape=out_shape,
        in_specs=[in_hbm] * len(inputs),
        out_specs=(in_vmem,) * len(outs),
        scratch_shapes=[
            *(pltpu.VMEM(value.shape, value.dtype) for value in inputs),
            pltpu.VMEM((half * slot_cap, row_count), bf16),
            pltpu.VMEM((half * base, row_count), bf16),
            pltpu.VMEM((over_cap, row_count), bf16),
            pltpu.VMEM(near_blocks, bf16),
            pltpu.VMEM(far_blocks, bf16),
            pltpu.VMEM((over_cap, features), bf16),
            pltpu.VMEM((16, over_cap), f32),
            pltpu.VMEM(near_blocks, bf16),
            pltpu.VMEM(far_blocks, bf16),
            pltpu.VMEM((over_cap, features), bf16),
            pltpu.VMEM((16, over_cap), f32),
            pltpu.VMEM(far_blocks, bf16),
            pltpu.VMEM(far_blocks, bf16),
            pltpu.VMEM(near_blocks, bf16),
            pltpu.VMEM(far_blocks, bf16),
            pltpu.VMEM(far_blocks, bf16),
            pltpu.VMEM(near_blocks, bf16),
            pltpu.VMEM(far_blocks, bf16),
            pltpu.VMEM(far_blocks, bf16),
            pltpu.VMEM((over_cap, features), bf16),
            pltpu.VMEM((over_cap, features), bf16),
            pltpu.VMEM((half * base, over_cap), bf16),
            pltpu.VMEM((slots, features), bf16),
            pltpu.VMEM((slots, latent_count), bf16),
            pltpu.VMEM((slots, features), bf16),
            pltpu.VMEM((slots, latent_count), bf16),
            pltpu.VMEM((row_count, features), f32),
            pltpu.VMEM((3, 1, features + 128), f32),
            pltpu.VMEM((half, 1, features + 128), f32),
            pltpu.SemaphoreType.DMA((len(inputs),)),
            *(pltpu.SemaphoreType.DMA((half,)) for _ in range(12)),
            pltpu.SemaphoreType.DMA((3,)),
            pltpu.SemaphoreType.DMA((3,)),
            pltpu.SemaphoreType.DMA((half,)),
            pltpu.SemaphoreType.DMA((half,)),
        ],
        compiler_params=pltpu.CompilerParams(
            collective_id=0, has_side_effects=True, vmem_limit_bytes=VMEM_LIMIT
        ),
        name="whole_step",
    )(*inputs)
    return results


def write_results(results):
    in_vmem = pl.BlockSpec(memory_space=pltpu.VMEM)
    anywhere = pl.BlockSpec(memory_space=pl.ANY)
    count = len(results)
    return pl.pallas_call(
        functools.partial(write_kernel, count),
        out_shape=tuple(pltpu.HBM(value.shape, value.dtype) for value in results),
        in_specs=[in_vmem] * count,
        out_specs=(anywhere,) * count,
        scratch_shapes=[pltpu.SemaphoreType.DMA((count,))],
        compiler_params=pltpu.CompilerParams(vmem_limit_bytes=1 << 20),
        name="write_results",
    )(*results)


def three_parts(values):
    high = values.astype(jnp.bfloat16).astype(jnp.float32)
    middle = (values - high).astype(jnp.bfloat16).astype(jnp.float32)
    low = values - high - middle
    row = lax.broadcasted_iota(jnp.int32, (16, values.shape[1]), 0)
    stacked = jnp.where(
        row == 0, high, jnp.where(row == 1, middle, jnp.where(row == 2, low, 0.0))
    )
    return stacked.astype(jnp.bfloat16)


def centre_kernel(devices, members, part_ref, total_ref, parts, send_sem, recv_sem):
    greet(devices, members)
    copies = []
    for offset in range(1, devices):
        copies.append(
            pltpu.make_async_remote_copy(
                src_ref=part_ref,
                dst_ref=parts.at[lax.axis_index("group") * members + lax.axis_index("member")],
                send_sem=send_sem.at[offset],
                recv_sem=recv_sem.at[offset],
                device_id=partner_of(offset, members),
                device_id_type=MESH,
            )
        )
        copies[-1].start()
    parts[lax.axis_index("group") * members + lax.axis_index("member")] = part_ref[...]
    for copy in copies:
        copy.wait_recv()
    total_ref[...] = jnp.sum(parts[...], axis=0)
    for copy in copies:
        copy.wait_send()


def centre_sum(part, devices, members):
    shape = (1, part.shape[0])
    return pl.pallas_call(
        functools.partial(centre_kernel, devices, members),
        out_shape=jax.ShapeDtypeStruct(shape, jnp.float32),
        in_specs=[pl.BlockSpec(memory_space=pltpu.VMEM)],
        out_specs=pl.BlockSpec(memory_space=pltpu.VMEM),
        scratch_shapes=[
            pltpu.VMEM((devices,) + shape, jnp.float32),
            pltpu.SemaphoreType.DMA((devices,)),
            pltpu.SemaphoreType.DMA((devices,)),
        ],
        compiler_params=pltpu.CompilerParams(
            collective_id=1, has_side_effects=True, vmem_limit_bytes=4 << 20
        ),
        name="centre_sum",
    )(part[None])[0]


def power_of_two(number):
    return number & (number - 1) == 0


def power_of_two(number):
    return number & (number - 1) == 0


def plain_step(
    activations,
    routes,
    centre_bias,
    centre_first,
    centre_second,
    router,
    router_first,
    router_second,
    encoder,
    enc_bias,
    decoder,
    encoder_first,
    encoder_second,
    enc_bias_first,
    enc_bias_second,
    decoder_first,
    decoder_second,
):
    groups = lax.axis_size("group")
    members = lax.axis_size("member")
    devices = groups * members
    row_count = activations.shape[0]
    feature_count = activations.shape[1]
    slot_cap = 2 * row_count // devices
    route_ids = routes[:, 0]
    onehot = (route_ids[:, None] == jnp.arange(devices, dtype=jnp.int32)[None, :]).astype(
        jnp.bfloat16
    )
    earlier = (jnp.arange(row_count)[:, None] > jnp.arange(row_count)[None, :]).astype(jnp.bfloat16)
    before = jnp.dot(earlier, onehot, preferred_element_type=jnp.float32)
    slot_rank = jnp.sum(before * onehot.astype(jnp.float32), axis=1).astype(jnp.int32)
    position = route_ids * slot_cap + slot_rank
    chosen = jnp.arange(devices * slot_cap, dtype=jnp.int32)[:, None] == position[None, :]
    select = chosen.astype(jnp.bfloat16)
    used = jnp.any(chosen, axis=1)
    packed = jnp.where(
        used[:, None],
        jnp.dot(select, activations, preferred_element_type=jnp.float32),
        EMPTY,
    ).astype(jnp.bfloat16)
    packed = packed.reshape(devices, slot_cap, feature_count)
    arrived = lax.all_to_all(
        packed, AXES, split_axis=0, concat_axis=0, tiled=True
    )
    in_rows = arrived.reshape(devices * slot_cap, feature_count)
    live_mask = (in_rows[:, 0] < 0.5 * EMPTY).astype(jnp.float32)
    centred, positive, latents, gating, ungated, rebuilt = forward_pass(
        in_rows, centre_bias, router[0], encoder[0], enc_bias[0], decoder[0]
    )
    outgoing = rebuilt.astype(jnp.bfloat16)
    returned = lax.all_to_all(
        outgoing.reshape(devices, slot_cap, feature_count),
        AXES,
        split_axis=0,
        concat_axis=0,
        tiled=True,
    )
    recon = lax.dot_general(
        select,
        returned.reshape(devices * slot_cap, feature_count),
        (((0,), (0,)), ((), ())),
        preferred_element_type=jnp.float32,
    ).astype(jnp.bfloat16)
    encoder_grad, bias_grad, decoder_grad, router_grad, centre_part = backward_pass(
        in_rows,
        live_mask,
        centred,
        positive,
        latents,
        gating,
        ungated,
        rebuilt,
        encoder[0],
        decoder[0],
    )
    router_new = adam_update(router[0], router_grad, router_first[0], router_second[0])
    encoder_new = adam_update(encoder[0], encoder_grad, encoder_first[0], encoder_second[0])
    bias_new = adam_update(enc_bias[0], bias_grad, enc_bias_first[0], enc_bias_second[0])
    decoder_new = adam_update(decoder[0], decoder_grad, decoder_first[0], decoder_second[0])
    if power_of_two(groups) and power_of_two(members):
        centre_part, first, second = lax.optimization_barrier(
            (centre_part, encoder_new[1], decoder_new[1])
        )
        encoder_new = (encoder_new[0], first, encoder_new[2])
        decoder_new = (decoder_new[0], second, decoder_new[2])
        centre_total = centre_sum(centre_part, devices, members)
    else:
        centre_total = lax.psum(centre_part, AXES)
    centre_new = adam_update(centre_bias, centre_total, centre_first, centre_second)
    return (
        recon,
        centre_new[0],
        centre_new[1],
        centre_new[2],
        router_new[0][None],
        router_new[1][None],
        router_new[2][None],
        encoder_new[0][None],
        bias_new[0][None],
        decoder_new[0][None],
        encoder_new[1][None],
        encoder_new[2][None],
        bias_new[1][None],
        bias_new[2][None],
        decoder_new[1][None],
        decoder_new[2][None],
    )


def per_device(*arrays):
    groups = lax.axis_size("group")
    members = lax.axis_size("member")
    devices = groups * members
    row_count, feature_count = arrays[0].shape
    slot_cap = 2 * row_count // devices
    aligned = slot_cap % 16 == 0 and power_of_two(groups) and power_of_two(members)
    aligned = aligned and members > 1 and row_count % 128 == 0 and row_count < 512
    aligned = aligned and feature_count % 128 == 0 and arrays[9].shape[1] % 128 == 0
    if not aligned:
        return plain_step(*arrays)
    operands = [value[0] if value.ndim == 3 else value for value in arrays[2:]]
    fast = whole_step(arrays[0], arrays[1], operands, members, devices)

    def keep(results, arrays):
        del arrays
        results = write_results(results)
        large = (7, 9, 10, 11, 14, 15)
        return tuple(
            value[None] if number in large else value for number, value in enumerate(results)
        )

    def again(results, arrays):
        del results
        return plain_step(*arrays)

    return lax.cond(fast[-1][0, 0] > 0.5, again, keep, fast[:-1], arrays)


def solution(mesh):
    placed = (
        P(AXES, None),
        P(AXES, None),
        P(),
        P(),
        P(),
        P(AXES, None),
        P(AXES, None),
        P(AXES, None),
        P(AXES, None, None),
        P(AXES, None),
        P(AXES, None, None),
        P(AXES, None, None),
        P(AXES, None, None),
        P(AXES, None),
        P(AXES, None),
        P(AXES, None, None),
        P(AXES, None, None),
    )
    return jax.shard_map(
        per_device,
        mesh=mesh,
        in_specs=placed,
        out_specs=(
            P(AXES, None),
            P(),
            P(),
            P(),
            P(AXES, None),
            P(AXES, None),
            P(AXES, None),
            P(AXES, None, None),
            P(AXES, None),
            P(AXES, None, None),
            P(AXES, None, None),
            P(AXES, None, None),
            P(AXES, None),
            P(AXES, None),
            P(AXES, None, None),
            P(AXES, None, None),
        ),
        check_vma=False,
    )
```

```python
import functools
import types

import jax
import jax.numpy as jnp
from jax import lax
from jax.experimental import pallas as pl
from jax.experimental.pallas import tpu as pltpu
from jax.sharding import PartitionSpec as P

MESH = pl.DeviceIdType.MESH
AXES = ("group", "member")

STEP = 10


learn_rate = 0.001
beta_one = 0.9
beta_two = 0.999
adam_eps = 1e-08
sparsity = 0.1
EMPTY = 16.0
VMEM_LIMIT = 40 << 20
HELD_BLOCKS = 8
EARLY_NEAR = 2


def adam_update(weights_in, gradient, moment_one, moment_two):
    first_new = beta_one * moment_one + (1.0 - beta_one) * gradient
    second_new = beta_two * moment_two + (1.0 - beta_two) * gradient * gradient
    first_hat = first_new / (1.0 - beta_one**STEP)
    second_hat = second_new / (1.0 - beta_two**STEP)
    stepped = weights_in.astype(jnp.float32) - learn_rate * first_hat / (
        jnp.sqrt(second_hat) + adam_eps
    )
    return (stepped.astype(weights_in.dtype), first_new, second_new)


def forward_pass(in_rows, centre_bias, router_row, encoder, enc_bias, decoder):
    centred = (in_rows.astype(jnp.float32) - centre_bias).astype(jnp.bfloat16)
    preact = jnp.dot(centred, encoder, preferred_element_type=jnp.float32) + enc_bias
    positive = jnp.maximum(preact, 0.0)
    latents = (positive * positive).astype(jnp.bfloat16)
    router_wide = jnp.broadcast_to(router_row[:, None], (router_row.shape[0], 128))
    logits = jnp.dot(in_rows, router_wide, preferred_element_type=jnp.float32)[:, 0]
    gating = jax.nn.sigmoid(logits)
    ungated = jnp.dot(latents, decoder, preferred_element_type=jnp.float32)
    rebuilt = centre_bias + gating[:, None] * ungated
    return (centred, positive, latents, gating, ungated, rebuilt)


def backward_pass(
    in_rows, live_mask, centred, positive, latents, gating, ungated, rebuilt, encoder, decoder
):
    errors = (in_rows.astype(jnp.float32) - rebuilt) * live_mask[:, None]
    backward = (-gating[:, None] * errors).astype(jnp.bfloat16)
    decoder_grad = jnp.dot(latents.T, backward, preferred_element_type=jnp.float32)
    latent_grad = jnp.dot(backward, decoder.T, preferred_element_type=jnp.float32) + sparsity
    preact_grad = (latent_grad * 2.0 * positive * live_mask[:, None]).astype(jnp.bfloat16)
    encoder_grad = jnp.dot(centred.T, preact_grad, preferred_element_type=jnp.float32)
    bias_grad = jnp.sum(preact_grad.astype(jnp.float32), axis=0)
    logit_grad = (-jnp.sum(errors * ungated, axis=1) * gating * (1.0 - gating)).astype(jnp.bfloat16)
    router_grad = jnp.dot(logit_grad, in_rows, preferred_element_type=jnp.float32)
    centre_part = -jnp.sum(errors, axis=0) - jnp.dot(
        encoder.astype(jnp.float32), bias_grad, precision=lax.Precision.HIGHEST
    )
    return (encoder_grad, bias_grad, decoder_grad, router_grad, centre_part)


def flipped(index, bits):
    result, place = index, 1
    while place <= bits:
        if bits & place:
            result = result + (1 - 2 * lax.rem(lax.div(index, place), 2)) * place
        place *= 2
    return result


def partner_of(offset, members):
    return (
        flipped(lax.axis_index("group"), offset // members),
        flipped(lax.axis_index("member"), offset % members),
    )


def greet(devices, members):
    barrier = pltpu.get_barrier_semaphore()
    for offset in range(1, devices):
        pl.semaphore_signal(
            barrier, inc=1, device_id=partner_of(offset, members), device_id_type=MESH
        )
    pl.semaphore_wait(barrier, devices - 1)


IN_NAMES = (
    "x",
    "routes",
    "centre",
    "centre_m",
    "centre_v",
    "router",
    "router_m",
    "router_v",
    "encoder",
    "bias",
    "decoder",
    "em",
    "ev",
    "bias_m",
    "bias_v",
    "dm",
    "dv",
)
OUT_NAMES = (
    "o_recon",
    "o_centre",
    "o_centre_m",
    "o_centre_v",
    "o_router",
    "o_router_m",
    "o_router_v",
    "o_encoder",
    "o_bias",
    "o_decoder",
    "o_encoder_m",
    "o_encoder_v",
    "o_bias_m",
    "o_bias_v",
    "o_decoder_m",
    "o_decoder_v",
    "o_flag",
)
SCRATCH_NAMES = (
    "near_sel",
    "far_sel",
    "over_sel",
    "near_out",
    "far_out",
    "over_out",
    "meta_out",
    "near_in",
    "far_in",
    "over_in",
    "meta_in",
    "relay_out",
    "relay_in",
    "near_back",
    "far_back",
    "over_back",
    "near_ret",
    "far_ret",
    "relay_back",
    "comp_out",
    "comp_in",
    "match",
    "centred_buf",
    "latents_buf",
    "backward_buf",
    "preact_buf",
    "recon_acc",
    "part_buf",
    "part_in",
    "local_sem",
    "near_send",
    "near_recv",
    "far_send",
    "far_recv",
    "relay_send",
    "relay_recv",
    "nback_send",
    "nback_recv",
    "fback_send",
    "fback_recv",
    "rback_send",
    "rback_recv",
    "over_send",
    "over_recv",
    "part_send",
    "part_recv",
)
REF_NAMES = (
    tuple(name + "_in" for name in IN_NAMES)
    + OUT_NAMES
    + IN_NAMES
    + SCRATCH_NAMES
)
LOAD_ORDER = (
    "routes",
    "x",
    "encoder",
    "decoder",
    "centre",
    "router",
    "bias",
    "dm",
    "dv",
    "em",
    "ev",
    "router_m",
    "router_v",
    "bias_m",
    "bias_v",
    "centre_m",
    "centre_v",
)


def adam_step(weights, gradient, moment_one, moment_two):
    first_new = beta_one * moment_one + (1.0 - beta_one) * gradient
    second_new = beta_two * moment_two + (1.0 - beta_two) * (gradient * gradient)
    scaled = first_new * (learn_rate / (1.0 - beta_one**STEP))
    root = jnp.sqrt(second_new * (1.0 / (1.0 - beta_two**STEP))) + adam_eps
    return (weights.astype(jnp.float32) - scaled / root, first_new, second_new)


def lane_count(values, weights):
    tall = jnp.broadcast_to(values, (16, values.shape[1])).astype(jnp.bfloat16)
    return jnp.dot(tall, weights, preferred_element_type=jnp.float32)[:1]


def picked(wanted, positions):
    line = lax.broadcasted_iota(jnp.int32, (wanted, 1), 0)
    return (line == positions).astype(jnp.float32)


def unpick(chosen, rows):
    return lax.dot_general(
        chosen, rows, (((0,), (0,)), ((), ())), preferred_element_type=jnp.float32
    )


def whole_kernel(devices, members, slot_cap, *refs):
    r = types.SimpleNamespace(**dict(zip(REF_NAMES, refs, strict=True)))
    half_members = members // 2
    half = devices // 2
    base = slot_cap // 2
    near = [offset for offset in range(devices) if not offset & half_members]
    per_chunk = min(half, max(1, 128 // slot_cap))
    starts = list(range(0, half, per_chunk))
    row_count, features = r.x.shape
    latent_count = r.bias.shape[1]
    over_cap = r.over_sel.shape[0]
    my_group, my_member = lax.axis_index("group"), lax.axis_index("member")
    me = my_group * members + my_member

    barrier = pltpu.get_barrier_semaphore()
    for offset in range(1, devices):
        pl.semaphore_signal(
            barrier, inc=1, device_id=partner_of(offset, members), device_id_type=MESH
        )
    loads = {}
    for number, name in enumerate(LOAD_ORDER):
        loads[name] = pltpu.make_async_copy(
            getattr(r, name + "_in"), getattr(r, name), r.local_sem.at[number]
        )
        loads[name].start()

    def ready(*wanted):
        for name in wanted:
            loads[name].wait()

    def remote(source, target, send_sem, recv_sem, offset):
        copy = pltpu.make_async_remote_copy(
            src_ref=source,
            dst_ref=target,
            send_sem=send_sem,
            recv_sem=recv_sem,
            device_id=partner_of(offset, members),
            device_id_type=MESH,
        )
        sent.append(copy)
        return copy

    sent = []

    ready("routes")
    route = r.routes[...]
    expert = lax.broadcasted_iota(jnp.int32, (devices, row_count), 0)
    onehot = (expert == route).astype(jnp.float32)
    before_row = lax.broadcasted_iota(jnp.int32, (row_count, row_count), 0)
    this_row = lax.broadcasted_iota(jnp.int32, (row_count, row_count), 1)
    earlier = (before_row < this_row).astype(jnp.bfloat16)
    before = jnp.dot(onehot.astype(jnp.bfloat16), earlier, preferred_element_type=jnp.float32)
    rank = jnp.sum(before * onehot, axis=0, keepdims=True).astype(jnp.int32)
    apart = lax.bitwise_xor(route, jnp.broadcast_to(me, route.shape))
    inner = lax.bitwise_and(apart, members - 1)
    outer = lax.shift_right_logical(apart, members.bit_length() - 1)
    is_far = inner >= half_members
    place = outer * half_members + lax.bitwise_and(inner, half_members - 1)
    is_over = is_far & (rank >= base)
    over_line = is_over.astype(jnp.float32)
    over_rank = lane_count(over_line, earlier).astype(jnp.int32)
    over_total = jnp.sum(over_line, axis=1, keepdims=True)
    flag = (over_total > over_cap).astype(jnp.float32)
    near_at = jnp.where(is_far, -1, place * slot_cap + rank)
    far_at = jnp.where(is_far & (rank < base), place * base + rank, -1)
    over_at = jnp.where(is_over, over_rank, -1)
    over_slot = jnp.where(is_over, place * base + rank - (base - 1), 0).astype(jnp.float32)

    ready("x")

    def packed(chosen, bottom):
        rows = jnp.dot(chosen.astype(jnp.bfloat16), r.x[...], preferred_element_type=jnp.float32)
        if bottom is None:
            return rows
        used = jnp.sum(chosen, axis=1, keepdims=True) > 0.5
        return jnp.where(used, rows, bottom)

    chosen = picked(over_cap, over_at)
    r.over_sel[...] = chosen.astype(jnp.bfloat16)
    r.over_out[...] = packed(chosen, None).astype(jnp.bfloat16)
    tall_slot = jnp.broadcast_to(over_slot, (16, row_count)).astype(jnp.bfloat16)
    r.meta_out[...] = lax.dot_general(
        tall_slot,
        r.over_sel[...],
        (((1,), (1,)), ((), ())),
        preferred_element_type=jnp.float32,
    )
    pl.semaphore_wait(barrier, devices - 1)
    rows_hop = remote(
        r.over_out, r.over_in, r.over_send.at[0], r.over_recv.at[0], half_members
    )
    meta_hop = remote(
        r.meta_out, r.meta_in, r.over_send.at[1], r.over_recv.at[1], half_members
    )
    meta_hop.start()
    rows_hop.start()

    near_go = [None] * half

    def near_pack(start):
        amount = per_chunk * slot_cap
        chosen = picked(amount, near_at - start * slot_cap)
        r.near_sel[pl.ds(start * slot_cap, amount)] = chosen.astype(jnp.bfloat16)
        rows = packed(chosen, EMPTY).reshape(per_chunk, slot_cap, features).astype(jnp.bfloat16)
        r.near_out[pl.ds(start, per_chunk)] = rows
        for number in range(start, start + per_chunk):
            if near[number] == 0:
                r.near_in[number] = rows[number - start]
                continue
            near_go[number] = remote(
                r.near_out.at[number],
                r.near_in.at[number],
                r.near_send.at[number],
                r.near_recv.at[number],
                near[number],
            )
            near_go[number].start()

    for start in starts[:EARLY_NEAR]:
        near_pack(start)

    chosen = picked(half * base, far_at)
    r.far_sel[...] = chosen.astype(jnp.bfloat16)
    r.far_out[...] = packed(chosen, EMPTY).reshape(half, base, features).astype(jnp.bfloat16)
    far_go = []
    for number, offset in enumerate(near):
        far_go.append(
            remote(
                r.far_out.at[number],
                r.far_in.at[number],
                r.far_send.at[number],
                r.far_recv.at[number],
                offset + half_members,
            )
        )
        far_go[-1].start()

    meta_hop.wait_recv()
    line = lax.broadcasted_iota(jnp.int32, (half * base, 1), 0).astype(jnp.float32)
    match = (line + 1.0 == r.meta_in[pl.ds(0, 1)]).astype(jnp.float32)
    taken = jnp.sum(match, axis=1, keepdims=True) > 0.5
    r.match[...] = match.astype(jnp.bfloat16)
    rows_hop.wait_recv()
    rows = jnp.dot(r.match[...], r.over_in[...], preferred_element_type=jnp.float32)
    rows = jnp.where(taken, rows, EMPTY).reshape(half, base, features).astype(jnp.bfloat16)
    r.relay_out[...] = rows
    relay_go = [None] * half
    for number, offset in enumerate(near):
        if offset == 0:
            r.relay_in[number] = rows[number]
            continue
        relay_go[number] = remote(
            r.relay_out.at[number],
            r.relay_in.at[number],
            r.relay_send.at[number],
            r.relay_recv.at[number],
            offset,
        )
        relay_go[number].start()
    for start in starts[EARLY_NEAR:]:
        near_pack(start)

    ready("centre", "router", "bias", "encoder", "decoder")
    centre = r.centre[...].reshape(1, features)
    router = r.router[...].astype(jnp.float32)
    bias = r.bias[...]
    sums = [
        jnp.zeros((1, features), jnp.float32),
        jnp.zeros((1, features), jnp.float32),
        jnp.zeros((1, latent_count), jnp.float32),
    ]

    def compute(wide, line, send_back):
        amount = wide.shape[0]
        live = (wide[:, :1] < 0.5 * EMPTY).astype(jnp.float32)
        gating = jax.nn.sigmoid(jnp.sum(wide * router, axis=1, keepdims=True))
        centred = (wide - centre).astype(jnp.bfloat16)
        preact = jnp.dot(centred, r.encoder[...], preferred_element_type=jnp.float32) + bias
        positive = jnp.maximum(preact, 0.0)
        latents = (positive * positive).astype(jnp.bfloat16)
        ungated = jnp.dot(latents, r.decoder[...], preferred_element_type=jnp.float32)
        rebuilt = centre + gating * ungated
        send_back(rebuilt)
        errors = (wide - rebuilt) * live
        backward = (-gating * errors).astype(jnp.bfloat16)
        latent_grad = (
            lax.dot_general(
                backward,
                r.decoder[...],
                (((1,), (1,)), ((), ())),
                preferred_element_type=jnp.float32,
            )
            + sparsity
        )
        preact_grad = (latent_grad * 2.0 * positive * live).astype(jnp.bfloat16)
        logit_grad = -jnp.sum(errors * ungated, axis=1, keepdims=True) * gating * (1.0 - gating)
        logit_grad = logit_grad.astype(jnp.bfloat16).astype(jnp.float32)
        sums[0] = sums[0] + jnp.sum(errors, axis=0, keepdims=True)
        sums[1] = sums[1] + jnp.sum(logit_grad * wide, axis=0, keepdims=True)
        sums[2] = sums[2] + jnp.sum(preact_grad.astype(jnp.float32), axis=0, keepdims=True)
        chunk = pl.ds(line, amount)
        r.centred_buf[chunk] = centred
        r.latents_buf[chunk] = latents
        r.backward_buf[chunk] = backward
        r.preact_buf[chunk] = preact_grad

    near_come, far_come, relay_come = [None] * half, [None] * half, [None] * half

    def near_chunk(start):
        numbers = range(start, start + per_chunk)
        for number in numbers:
            if near_go[number] is not None:
                near_go[number].wait_recv()
        wide = r.near_in[pl.ds(start, per_chunk)].reshape(per_chunk * slot_cap, features)

        def send_back(rebuilt):
            r.near_back[pl.ds(start, per_chunk)] = rebuilt.astype(jnp.bfloat16).reshape(
                per_chunk, slot_cap, features
            )
            for number in numbers:
                if near[number] == 0:
                    r.near_ret[number] = r.near_back[number]
                    continue
                near_come[number] = remote(
                    r.near_back.at[number],
                    r.near_ret.at[number],
                    r.nback_send.at[number],
                    r.nback_recv.at[number],
                    near[number],
                )
                near_come[number].start()

        compute(wide.astype(jnp.float32), start * slot_cap, send_back)

    def passed_chunk():
        for copy in relay_go:
            if copy is not None:
                copy.wait_recv()
        wide = r.relay_in[...].astype(jnp.float32).reshape(half * base, features)

        def send_back(rebuilt):
            r.over_back[...] = rebuilt.reshape(half, base, features).astype(jnp.bfloat16)
            for number, offset in enumerate(near):
                if offset == 0:
                    r.relay_back[number] = r.over_back[number]
                    continue
                relay_come[number] = remote(
                    r.over_back.at[number],
                    r.relay_back.at[number],
                    r.rback_send.at[number],
                    r.rback_recv.at[number],
                    offset,
                )
                relay_come[number].start()

        compute(wide, half * slot_cap, send_back)

    def direct_chunk(start, count):
        numbers = range(start, start + count)
        for number in numbers:
            far_go[number].wait_recv()
        wide = r.far_in[pl.ds(start, count)].astype(jnp.float32).reshape(count * base, features)

        def send_back(rebuilt):
            r.far_back[pl.ds(start, count)] = rebuilt.reshape(count, base, features).astype(
                jnp.bfloat16
            )
            for number in numbers:
                far_come[number] = remote(
                    r.far_back.at[number],
                    r.far_ret.at[number],
                    r.fback_send.at[number],
                    r.fback_recv.at[number],
                    near[number] + half_members,
                )
                if number < half - HELD_BLOCKS:
                    far_come[number].start()

        compute(wide, half * slot_cap + (half + start) * base, send_back)

    def pass_back():
        for copy in relay_come:
            if copy is not None:
                copy.wait_recv()
        back = r.relay_back[...].astype(jnp.float32).reshape(half * base, features)
        back = back.astype(jnp.bfloat16)
        r.comp_out[...] = unpick(r.match[...], back).astype(jnp.bfloat16)
        hop = remote(r.comp_out, r.comp_in, r.over_send.at[2], r.over_recv.at[2], half_members)
        hop.start()
        return hop

    for start in starts:
        near_chunk(start)
    direct_chunk(0, half // 2)
    direct_chunk(half // 2, half // 2)
    passed_chunk()
    for number in range(half - HELD_BLOCKS, half - 1):
        far_come[number].start()
    error_sum, router_grad, bias_grad = sums
    products = lax.dot_general(
        three_parts(bias_grad),
        r.encoder[...],
        (((1,), (1,)), ((), ())),
        preferred_element_type=jnp.float32,
    )
    part = -error_sum - jnp.sum(products, axis=0, keepdims=True)
    part = jnp.concatenate([part, jnp.broadcast_to(flag, (1, 128))], axis=1)
    r.part_buf[0] = part
    my_place = my_group * half_members + lax.rem(my_member, half_members)
    parts = [None] * half
    for number, offset in enumerate(near):
        if offset:
            parts[number] = remote(
                r.part_buf.at[0],
                r.part_in.at[my_place],
                r.part_send.at[number],
                r.part_recv.at[number],
                offset,
            )
            parts[number].start()
    r.part_in[my_place] = part

    def adam_rows(index, left, right, weights, first, second, outs):
        lanes = pl.ds(pl.multiple_of(index * 128, 128), 128)
        gradient = unpick(left[:, lanes], right[...])
        stepped, first_new, second_new = adam_step(
            weights[lanes], gradient, first[lanes], second[lanes]
        )
        outs[0][lanes] = stepped.astype(outs[0].dtype)
        outs[1][lanes] = first_new
        outs[2][lanes] = second_new

    def decoder_rows(index, carry):
        outs = (r.o_decoder, r.o_decoder_m, r.o_decoder_v)
        adam_rows(index, r.latents_buf, r.backward_buf, r.decoder, r.dm, r.dv, outs)
        return carry

    def encoder_rows(index, carry):
        outs = (r.o_encoder, r.o_encoder_m, r.o_encoder_v)
        adam_rows(index, r.centred_buf, r.preact_buf, r.encoder, r.em, r.ev, outs)
        return carry

    for copy in near_come:
        if copy is not None:
            copy.wait_recv()
    r.recon_acc[...] = unpick(
        r.near_sel[...], r.near_ret[...].reshape(half * slot_cap, features)
    )
    for copy in parts:
        if copy is not None:
            copy.wait_recv()
    r.part_buf[1] = jnp.sum(r.part_in[...], axis=0)
    mirror = remote(
        r.part_buf.at[1], r.part_buf.at[2], r.part_send.at[0], r.part_recv.at[0], half_members
    )
    mirror.start()
    for number in range(half - 1, half):
        far_come[number].start()
    comp_hop = pass_back()

    ready("dm", "dv")
    lax.fori_loop(0, latent_count // 128, decoder_rows, 0)
    ready("em", "ev", "router_m", "router_v", "bias_m", "bias_v", "centre_m", "centre_v")
    lax.fori_loop(0, features // 128, encoder_rows, 0)
    stepped, r.o_router_m[...], r.o_router_v[...] = adam_step(
        r.router[...], router_grad, r.router_m[...], r.router_v[...]
    )
    r.o_router[...] = stepped.astype(r.o_router.dtype)
    r.o_bias[...], r.o_bias_m[...], r.o_bias_v[...] = adam_step(
        bias, bias_grad, r.bias_m[...], r.bias_v[...]
    )
    mirror.wait_recv()
    total = r.part_buf[1] + r.part_buf[2]
    r.o_flag[...] = total[:, features:]
    stepped, first_new, second_new = adam_step(
        centre,
        total[:, :features],
        r.centre_m[...].reshape(1, features),
        r.centre_v[...].reshape(1, features),
    )
    r.o_centre[...] = stepped.reshape(features)
    r.o_centre_m[...] = first_new.reshape(features)
    r.o_centre_v[...] = second_new.reshape(features)
    for copy in far_come:
        copy.wait_recv()
    back = r.far_ret[...].astype(jnp.float32).reshape(half * base, features)
    r.recon_acc[...] = r.recon_acc[...] + unpick(r.far_sel[...], back.astype(jnp.bfloat16))
    comp_hop.wait_recv()
    recon = r.recon_acc[...] + unpick(r.over_sel[...], r.comp_in[...])
    r.o_recon[...] = recon.astype(jnp.bfloat16)
    for copy in sent:
        copy.wait_send()


def write_kernel(count, *refs):
    sems = refs[-1]
    copies = []
    for number in range(count):
        copies.append(
            pltpu.make_async_copy(refs[number], refs[count + number], sems.at[number])
        )
        copies[-1].start()
    for copy in copies:
        copy.wait()


def whole_step(rows, routes, operands, members, devices):
    row_count, features = rows.shape
    encoder = operands[6]
    latent_count = encoder.shape[1]
    slot_cap = 2 * row_count // devices
    slots = devices * slot_cap
    inputs = tuple(
        pltpu.with_memory_space_constraint(value, pltpu.HBM)
        for value in (rows, routes.reshape(1, row_count), *operands)
    )
    in_vmem = pl.BlockSpec(memory_space=pltpu.VMEM)
    in_hbm = pl.BlockSpec(memory_space=pltpu.HBM)
    bf16, f32 = jnp.bfloat16, jnp.float32
    by_feature, by_latent = (features, latent_count), (latent_count, features)
    outs = [
        ((row_count, features), bf16),
        ((features,), f32),
        ((features,), f32),
        ((features,), f32),
        ((1, features), bf16),
        ((1, features), f32),
        ((1, features), f32),
        (by_feature, bf16),
        ((1, latent_count), f32),
        (by_latent, bf16),
        (by_feature, f32),
        (by_feature, f32),
        ((1, latent_count), f32),
        ((1, latent_count), f32),
        (by_latent, f32),
        (by_latent, f32),
        ((1, 128), f32),
    ]
    out_shape = tuple(jax.ShapeDtypeStruct(shape, dtype) for shape, dtype in outs)
    half, base = devices // 2, slot_cap // 2
    over_cap = slots // 8
    near_blocks = (half, slot_cap, features)
    far_blocks = (half, base, features)
    results = pl.pallas_call(
        functools.partial(whole_kernel, devices, members, slot_cap),
        out_shape=out_shape,
        in_specs=[in_hbm] * len(inputs),
        out_specs=(in_vmem,) * len(outs),
        scratch_shapes=[
            *(pltpu.VMEM(value.shape, value.dtype) for value in inputs),
            pltpu.VMEM((half * slot_cap, row_count), bf16),
            pltpu.VMEM((half * base, row_count), bf16),
            pltpu.VMEM((over_cap, row_count), bf16),
            pltpu.VMEM(near_blocks, bf16),
            pltpu.VMEM(far_blocks, bf16),
            pltpu.VMEM((over_cap, features), bf16),
            pltpu.VMEM((16, over_cap), f32),
            pltpu.VMEM(near_blocks, bf16),
            pltpu.VMEM(far_blocks, bf16),
            pltpu.VMEM((over_cap, features), bf16),
            pltpu.VMEM((16, over_cap), f32),
            pltpu.VMEM(far_blocks, bf16),
            pltpu.VMEM(far_blocks, bf16),
            pltpu.VMEM(near_blocks, bf16),
            pltpu.VMEM(far_blocks, bf16),
            pltpu.VMEM(far_blocks, bf16),
            pltpu.VMEM(near_blocks, bf16),
            pltpu.VMEM(far_blocks, bf16),
            pltpu.VMEM(far_blocks, bf16),
            pltpu.VMEM((over_cap, features), bf16),
            pltpu.VMEM((over_cap, features), bf16),
            pltpu.VMEM((half * base, over_cap), bf16),
            pltpu.VMEM((slots, features), bf16),
            pltpu.VMEM((slots, latent_count), bf16),
            pltpu.VMEM((slots, features), bf16),
            pltpu.VMEM((slots, latent_count), bf16),
            pltpu.VMEM((row_count, features), f32),
            pltpu.VMEM((3, 1, features + 128), f32),
            pltpu.VMEM((half, 1, features + 128), f32),
            pltpu.SemaphoreType.DMA((len(inputs),)),
            *(pltpu.SemaphoreType.DMA((half,)) for _ in range(12)),
            pltpu.SemaphoreType.DMA((3,)),
            pltpu.SemaphoreType.DMA((3,)),
            pltpu.SemaphoreType.DMA((half,)),
            pltpu.SemaphoreType.DMA((half,)),
        ],
        compiler_params=pltpu.CompilerParams(
            collective_id=0, has_side_effects=True, vmem_limit_bytes=VMEM_LIMIT
        ),
        name="whole_step",
    )(*inputs)
    return results


def write_results(results):
    in_vmem = pl.BlockSpec(memory_space=pltpu.VMEM)
    anywhere = pl.BlockSpec(memory_space=pl.ANY)
    count = len(results)
    return pl.pallas_call(
        functools.partial(write_kernel, count),
        out_shape=tuple(pltpu.HBM(value.shape, value.dtype) for value in results),
        in_specs=[in_vmem] * count,
        out_specs=(anywhere,) * count,
        scratch_shapes=[pltpu.SemaphoreType.DMA((count,))],
        compiler_params=pltpu.CompilerParams(vmem_limit_bytes=1 << 20),
        name="write_results",
    )(*results)


def three_parts(values):
    high = values.astype(jnp.bfloat16).astype(jnp.float32)
    middle = (values - high).astype(jnp.bfloat16).astype(jnp.float32)
    low = values - high - middle
    row = lax.broadcasted_iota(jnp.int32, (16, values.shape[1]), 0)
    stacked = jnp.where(
        row == 0, high, jnp.where(row == 1, middle, jnp.where(row == 2, low, 0.0))
    )
    return stacked.astype(jnp.bfloat16)


def centre_kernel(devices, members, part_ref, total_ref, parts, send_sem, recv_sem):
    greet(devices, members)
    copies = []
    for offset in range(1, devices):
        copies.append(
            pltpu.make_async_remote_copy(
                src_ref=part_ref,
                dst_ref=parts.at[lax.axis_index("group") * members + lax.axis_index("member")],
                send_sem=send_sem.at[offset],
                recv_sem=recv_sem.at[offset],
                device_id=partner_of(offset, members),
                device_id_type=MESH,
            )
        )
        copies[-1].start()
    parts[lax.axis_index("group") * members + lax.axis_index("member")] = part_ref[...]
    for copy in copies:
        copy.wait_recv()
    total_ref[...] = jnp.sum(parts[...], axis=0)
    for copy in copies:
        copy.wait_send()


def centre_sum(part, devices, members):
    shape = (1, part.shape[0])
    return pl.pallas_call(
        functools.partial(centre_kernel, devices, members),
        out_shape=jax.ShapeDtypeStruct(shape, jnp.float32),
        in_specs=[pl.BlockSpec(memory_space=pltpu.VMEM)],
        out_specs=pl.BlockSpec(memory_space=pltpu.VMEM),
        scratch_shapes=[
            pltpu.VMEM((devices,) + shape, jnp.float32),
            pltpu.SemaphoreType.DMA((devices,)),
            pltpu.SemaphoreType.DMA((devices,)),
        ],
        compiler_params=pltpu.CompilerParams(
            collective_id=1, has_side_effects=True, vmem_limit_bytes=4 << 20
        ),
        name="centre_sum",
    )(part[None])[0]


def power_of_two(number):
    return number & (number - 1) == 0


def power_of_two(number):
    return number & (number - 1) == 0


def plain_step(
    activations,
    routes,
    centre_bias,
    centre_first,
    centre_second,
    router,
    router_first,
    router_second,
    encoder,
    enc_bias,
    decoder,
    encoder_first,
    encoder_second,
    enc_bias_first,
    enc_bias_second,
    decoder_first,
    decoder_second,
):
    groups = lax.axis_size("group")
    members = lax.axis_size("member")
    devices = groups * members
    row_count = activations.shape[0]
    feature_count = activations.shape[1]
    slot_cap = 2 * row_count // devices
    route_ids = routes[:, 0]
    onehot = (route_ids[:, None] == jnp.arange(devices, dtype=jnp.int32)[None, :]).astype(
        jnp.bfloat16
    )
    earlier = (jnp.arange(row_count)[:, None] > jnp.arange(row_count)[None, :]).astype(jnp.bfloat16)
    before = jnp.dot(earlier, onehot, preferred_element_type=jnp.float32)
    slot_rank = jnp.sum(before * onehot.astype(jnp.float32), axis=1).astype(jnp.int32)
    position = route_ids * slot_cap + slot_rank
    chosen = jnp.arange(devices * slot_cap, dtype=jnp.int32)[:, None] == position[None, :]
    select = chosen.astype(jnp.bfloat16)
    used = jnp.any(chosen, axis=1)
    packed = jnp.where(
        used[:, None],
        jnp.dot(select, activations, preferred_element_type=jnp.float32),
        EMPTY,
    ).astype(jnp.bfloat16)
    packed = packed.reshape(devices, slot_cap, feature_count)
    arrived = lax.all_to_all(
        packed, AXES, split_axis=0, concat_axis=0, tiled=True
    )
    in_rows = arrived.reshape(devices * slot_cap, feature_count)
    live_mask = (in_rows[:, 0] < 0.5 * EMPTY).astype(jnp.float32)
    centred, positive, latents, gating, ungated, rebuilt = forward_pass(
        in_rows, centre_bias, router[0], encoder[0], enc_bias[0], decoder[0]
    )
    outgoing = rebuilt.astype(jnp.bfloat16)
    returned = lax.all_to_all(
        outgoing.reshape(devices, slot_cap, feature_count),
        AXES,
        split_axis=0,
        concat_axis=0,
        tiled=True,
    )
    recon = lax.dot_general(
        select,
        returned.reshape(devices * slot_cap, feature_count),
        (((0,), (0,)), ((), ())),
        preferred_element_type=jnp.float32,
    ).astype(jnp.bfloat16)
    encoder_grad, bias_grad, decoder_grad, router_grad, centre_part = backward_pass(
        in_rows,
        live_mask,
        centred,
        positive,
        latents,
        gating,
        ungated,
        rebuilt,
        encoder[0],
        decoder[0],
    )
    router_new = adam_update(router[0], router_grad, router_first[0], router_second[0])
    encoder_new = adam_update(encoder[0], encoder_grad, encoder_first[0], encoder_second[0])
    bias_new = adam_update(enc_bias[0], bias_grad, enc_bias_first[0], enc_bias_second[0])
    decoder_new = adam_update(decoder[0], decoder_grad, decoder_first[0], decoder_second[0])
    if power_of_two(groups) and power_of_two(members):
        centre_part, first, second = lax.optimization_barrier(
            (centre_part, encoder_new[1], decoder_new[1])
        )
        encoder_new = (encoder_new[0], first, encoder_new[2])
        decoder_new = (decoder_new[0], second, decoder_new[2])
        centre_total = centre_sum(centre_part, devices, members)
    else:
        centre_total = lax.psum(centre_part, AXES)
    centre_new = adam_update(centre_bias, centre_total, centre_first, centre_second)
    return (
        recon,
        centre_new[0],
        centre_new[1],
        centre_new[2],
        router_new[0][None],
        router_new[1][None],
        router_new[2][None],
        encoder_new[0][None],
        bias_new[0][None],
        decoder_new[0][None],
        encoder_new[1][None],
        encoder_new[2][None],
        bias_new[1][None],
        bias_new[2][None],
        decoder_new[1][None],
        decoder_new[2][None],
    )


def per_device(*arrays):
    groups = lax.axis_size("group")
    members = lax.axis_size("member")
    devices = groups * members
    row_count, feature_count = arrays[0].shape
    slot_cap = 2 * row_count // devices
    aligned = slot_cap % 16 == 0 and power_of_two(groups) and power_of_two(members)
    aligned = aligned and members > 1 and row_count % 128 == 0 and row_count < 512
    aligned = aligned and feature_count % 128 == 0 and arrays[9].shape[1] % 128 == 0
    if not aligned:
        return plain_step(*arrays)
    operands = [value[0] if value.ndim == 3 else value for value in arrays[2:]]
    fast = whole_step(arrays[0], arrays[1], operands, members, devices)

    def keep(results, arrays):
        del arrays
        results = write_results(results)
        large = (7, 9, 10, 11, 14, 15)
        return tuple(
            value[None] if number in large else value for number, value in enumerate(results)
        )

    def again(results, arrays):
        del results
        return plain_step(*arrays)

    return lax.cond(fast[-1][0, 0] > 0.5, again, keep, fast[:-1], arrays)


def solution(mesh):
    placed = (
        P(AXES, None),
        P(AXES, None),
        P(),
        P(),
        P(),
        P(AXES, None),
        P(AXES, None),
        P(AXES, None),
        P(AXES, None, None),
        P(AXES, None),
        P(AXES, None, None),
        P(AXES, None, None),
        P(AXES, None, None),
        P(AXES, None),
        P(AXES, None),
        P(AXES, None, None),
        P(AXES, None, None),
    )
    return jax.shard_map(
        per_device,
        mesh=mesh,
        in_specs=placed,
        out_specs=(
            P(AXES, None),
            P(),
            P(),
            P(),
            P(AXES, None),
            P(AXES, None),
            P(AXES, None),
            P(AXES, None, None),
            P(AXES, None),
            P(AXES, None, None),
            P(AXES, None, None),
            P(AXES, None, None),
            P(AXES, None),
            P(AXES, None),
            P(AXES, None, None),
            P(AXES, None, None),
        ),
        check_vma=False,
    )
```
